256 devices in a mesh: tm: 32 (over y, z_hi, x), head: 8 (over z_lo, core).
Axes of the slice: x: 4, y: 4, z: 8 (z_hi: 2, z_lo: 4; z = z_hi * 4 + z_lo), core: 2. Of those that a mesh axis runs over, the one named last changes fastest.
Arguments:
- queries: bfloat16 [4096, 6144], P('tm', 'head'), may hold values from -150 to 150
- window_keys: bfloat16 [4096, 6144], P('tm', 'head'), may hold values from -6 to 6
- window_values: bfloat16 [4096, 6144], P('tm', 'head'), may hold values from -6 to 6
- context_keys: bfloat16 [4096, 6144], P('tm', 'head'), may hold values from -6 to 6
- context_values: bfloat16 [4096, 6144], P('tm', 'head'), may hold values from -6 to 6
- block_group: int32 [128], replicated, may hold values from 0 to 31, never falling along the last dimension, each value on 1 to 8 neighbouring positions
- sees: int32 [32, 32], replicated, may hold values from 0 to 1, as said below
- out_weight: bfloat16 [6144, 6144], P('head'), may hold values from -1 to 1
- gate: float32 [6144], P('head'), may hold values from 0.5 to 2
Outputs:
- update: bfloat16 [4096, 6144], P('tm', 'head')
The draws below stay inside these ranges and needn't reach their ends.
Inputs may be any that keep to these rules, and one draw needn't show every extreme that they name: sees[a, a] is 1 and sees[a, b] is 0 for b > a. `block_group`: never falling along the blocks.
All inputs are finite; a program needn't handle non-finite values.
Results may differ from the reference program's by a relative error of at most 0.03.
Values may be sent and summed in bfloat16 or wider, within the bound.
A program may use at most 128 MiB of HBM per device.

```python
import math
import jax
import jax.numpy as jnp
import numpy as np
from jax import lax

HEADS = 48
HD = 128
D = 6144
BLOCK = 64
WIN = 4096
CTX = 4096
NBLK = 128
NCHUNK = 32


def pair_draw(key):
    query_key = jax.random.fold_in(key, 11)
    window_key = jax.random.fold_in(key, 12)
    keys_drawn = jnp.clip(jax.random.normal(window_key, (WIN, D), jnp.float32), -6.0, 6.0)
    queries_drawn = jnp.clip(jax.random.normal(query_key, (WIN, D), jnp.float32), -6.0, 6.0)
    return (queries_drawn, keys_drawn)


def draw_queries(key, part):
    return pair_draw(key)[0].astype(jnp.bfloat16)


def draw_window_keys(key, part):
    return pair_draw(key)[1].astype(jnp.bfloat16)


def draw_sees(key, part):
    coins = jax.random.randint(jax.random.fold_in(key, 21), (NCHUNK, NCHUNK), 0, 4)
    row_ids = jnp.arange(NCHUNK, dtype=jnp.int32)[:, None]
    col_ids = jnp.arange(NCHUNK, dtype=jnp.int32)[None, :]
    lower = jnp.where(coins != 0, 1, 0).astype(jnp.int32)
    return jnp.where(row_ids == col_ids, 1, jnp.where(row_ids > col_ids, lower, 0)).astype(jnp.int32)


def shard_levels(own_key, dims, pieces, low, high):
    def one(dim, parts):
        heights = jax.random.uniform(jax.random.fold_in(jax.random.fold_in(own_key, 6), dim), (parts,), jnp.float32, low / len(pieces), high / len(pieces))
        return jnp.repeat(jnp.exp(heights), dims[dim] // parts).reshape((-1,) + (1,) * (len(dims) - dim - 1))

    level = one(*pieces[0])
    for cut in pieces[1:]:
        level = level * one(*cut)
    return level


def split_up(amount, total, reach, slope):
    weights = [(1 << 20) // math.isqrt(grade ** slope) + 1 for grade in range(2, amount + 1)]
    spare, given = total - reach - (amount - 1), [1] * (amount - 1)
    while spare > 0:
        movable = [i for i in range(amount - 1) if given[i] < reach]
        pool, left = sum([weights[i] for i in movable]), spare
        for i in movable:
            more = min(reach - given[i], max(1, left * weights[i] // pool), spare)
            given[i] = given[i] + more
            spare = spare - more
    return np.array([reach] + given)


def uneven_parts(stream_key, amount, total, most, lean):
    if amount == 2:
        one = jax.random.randint(stream_key, (), max(1, total - most), min(most, total - 1) + 1)
        return jnp.stack([one, total - one])
    sizes = jnp.asarray(split_up(amount, total, most, lean), jnp.int32)
    couples = (amount - 1) // 2
    donor, taker = sizes[1:1 + 2 * couples:2], sizes[2:2 + 2 * couples:2]
    room = jnp.minimum(donor - 1, most - taker)
    passed = jax.random.randint(jax.random.fold_in(stream_key, 1), (couples,), 0, 1 << 20) % (room + 1)
    sizes = sizes.at[1:1 + 2 * couples:2].set(donor - passed).at[2:2 + 2 * couples:2].set(taker + passed)
    return sizes[jax.random.permutation(jax.random.fold_in(stream_key, 2), amount)]


def centred(own_key, shape, width, most, cuts=(), held_as=jnp.bfloat16):
    drawn = jax.random.normal(own_key, shape, jnp.float32) * width
    if len(cuts) > 0:
        drawn = shard_levels(own_key, shape, cuts, -0.22, 0.18) * drawn
    return jnp.clip(drawn, min=-most, max=most).astype(held_as)


def setup_inputs(seed: int = 0) -> dict:
    arg_keys = jax.random.split(jax.random.key(seed), 10)
    return {
        "queries": draw_queries(jax.random.fold_in(arg_keys[9], 71), 0),
        "window_keys": draw_window_keys(jax.random.fold_in(arg_keys[9], 71), 0),
        "window_values": centred(arg_keys[2], (WIN, D), 1.0, 6.0, ((0, 32), (1, 8))),
        "context_keys": centred(arg_keys[3], (CTX, D), 1.0, 6.0, ((0, 32), (1, 8))),
        "context_values": centred(arg_keys[4], (CTX, D), 1.0, 6.0, ((0, 32), (1, 8))),
        "block_group": jnp.searchsorted(jnp.cumsum(uneven_parts(arg_keys[5], NCHUNK, NBLK, 8, 1)), jnp.arange(NBLK), side="right").astype(jnp.int32),
        "sees": draw_sees(jax.random.fold_in(arg_keys[9], 71), 0),
        "out_weight": centred(arg_keys[7], (D, D), (HD // 4) ** -0.5, 1.0, ((0, 8),)),
        "gate": jnp.clip(0.5 + 1.5 * jax.random.uniform(arg_keys[8], (D,), jnp.float32) ** shard_levels(arg_keys[8], (D,), ((0, 8),), -0.2, 0.2), 0.5, 2.0),
    }


def group_mask(block_group, sees):
    positions = jnp.arange(CTX + WIN, dtype=jnp.int32)
    key_groups = block_group[positions // BLOCK]
    query_groups = key_groups[CTX:]
    return sees[query_groups][:, key_groups] > 0

def reference(queries, window_keys, window_values, context_keys, context_values, block_group, sees, out_weight, gate):
    all_keys = jnp.concatenate([context_keys, window_keys], axis=0)
    all_values = jnp.concatenate([context_values, window_values], axis=0)
    visible = group_mask(block_group, sees)
    score_scale = 1.0 / jnp.sqrt(jnp.float32(HD))

    def one_head(head_id):
        start = (head_id * HD).astype(jnp.int32)
        query_h = lax.dynamic_slice_in_dim(queries, start, HD, 1)
        key_h = lax.dynamic_slice_in_dim(all_keys, start, HD, 1)
        value_h = lax.dynamic_slice_in_dim(all_values, start, HD, 1)
        scores = jnp.dot(query_h, key_h.T, preferred_element_type=jnp.float32) * score_scale
        scores = jnp.where(visible, scores, jnp.float32(-1e+30))
        row_peak = lax.optimization_barrier(jnp.max(scores, axis=-1, keepdims=True))
        weights = jnp.where(visible, jnp.exp(scores - row_peak), jnp.float32(0.0))
        row_total = lax.optimization_barrier(jnp.sum(weights, axis=-1, keepdims=True))
        numer = jnp.dot(weights.astype(jnp.bfloat16), value_h, preferred_element_type=jnp.float32)
        return (numer / row_total).astype(jnp.bfloat16)
    per_head = lax.map(one_head, jnp.arange(HEADS, dtype=jnp.int32))
    attended = jnp.transpose(per_head, (1, 0, 2)).reshape(WIN, D)
    projected = jnp.dot(attended, out_weight, preferred_element_type=jnp.float32)
    return (gate[None, :] * projected).astype(jnp.bfloat16)
```

```python
import functools
import math

import jax
import jax.numpy as jnp
from jax import lax
from jax.experimental import pallas as pl
from jax.experimental.pallas import tpu as pltpu
from jax.sharding import PartitionSpec as P

HD = 128
BLOCK = 64
ROWS = 128
NH = 6
FEAT = NH * HD
RING = 4
KEYS = 2 * ROWS * RING
KB = KEYS // BLOCK
QCH = 2 * RING
MSG = HD + 16
HEADS_Z = 4
NBLK = 128
SUB = 2
SUBR = ROWS // SUB
BIG = 1e30
FLOOR = -1e29
MESH = pl.DeviceIdType.MESH
LOG2 = math.log2(math.e) / math.sqrt(HD)


def remote(src, dst, send, recv, **device):
    return pltpu.make_async_remote_copy(
        src_ref=src, dst_ref=dst, send_sem=send, recv_sem=recv, device_id=device, device_id_type=MESH
    )


class Plan:
    def __init__(self, *entries):
        self.entries = entries

    def __getitem__(self, index):
        src, dst, send, recv, peer = self.entries[index]
        return remote(src, dst, send, recv, tm=peer)

    def __len__(self):
        return len(self.entries)


def dot_nt(a, b):
    return lax.dot_general(a, b, (((1,), (1,)), ((), ())), preferred_element_type=jnp.float32)


def unpack(message):
    stats = message[HD:MSG, :].astype(jnp.float32)
    return (message[0:HD, :].astype(jnp.float32), stats[0:1, :], stats[1:2, :] + stats[2:3, :])


def merge(parts):
    peak = parts[0][1]
    for part in parts[1:]:
        peak = jnp.maximum(peak, part[1])
    numer = None
    total = None
    for part in parts:
        factor = jnp.exp2(part[1] - peak)
        numer = part[0] * factor if numer is None else numer + part[0] * factor
        total = part[2] * factor if total is None else total + part[2] * factor
    return (numer, peak, total)


def stat_rows(peak, total):
    high = total.astype(jnp.bfloat16).astype(jnp.float32)
    rows = lax.broadcasted_iota(jnp.int32, (MSG - HD, peak.shape[1]), 0)
    picked = jnp.where(rows == 0, peak, jnp.where(rows == 1, high, total - high))
    return picked.astype(jnp.bfloat16)


def kernel(
    q_hbm,
    wk_hbm,
    wv_hbm,
    ck_hbm,
    cv_hbm,
    group_ref,
    sees_ref,
    w_hbm,
    gate_ref,
    out_ref,
    qbuf,
    kbuf,
    vbuf,
    vt,
    pen,
    pbuf,
    ibuf,
    att,
    wbuf,
    pst,
    pin,
    own,
    rst,
    rin,
    load_sem,
    w_sem,
    kv_send,
    kv_recv,
    q_send,
    q_recv,
    o_send,
    o_recv,
    p_send,
    p_recv,
    r_send,
    r_recv,
):
    t = lax.axis_index("tm")
    hd = lax.axis_index("head")
    x = t % 4
    s = (t // 4) % 2
    y = t // 8
    zl = hd // 2
    core = hd % 2
    flip = t + 4 - 8 * s
    other = hd + 1 - 2 * core

    def along(delta):
        return (t - x + (x + delta + 4) % 4, t + ((y + delta + 4) % 4 - y) * 8)

    x_up, y_up = along(1)
    x_down, y_down = along(-1)

    def kv_peer(par, up):
        a, b = (x_up, y_up) if up else (x_down, y_down)
        return a * (1 - par) + b * par

    def q_peer(par, up):
        a, b = (x_up, y_up) if up else (x_down, y_down)
        return a * par + b * (1 - par)

    def loads(h):
        cols = pl.ds(pl.multiple_of(h * HD, HD), HD)
        return (
            pltpu.make_async_copy(q_hbm.at[:, cols], qbuf.at[h, 0:ROWS], load_sem.at[h, 0]),
            pltpu.make_async_copy(ck_hbm.at[:, cols], kbuf.at[h, 0:ROWS], load_sem.at[h, 1]),
            pltpu.make_async_copy(wk_hbm.at[:, cols], kbuf.at[h, ROWS : 2 * ROWS], load_sem.at[h, 2]),
            pltpu.make_async_copy(cv_hbm.at[:, cols], vbuf.at[h, 0:ROWS], load_sem.at[h, 3]),
            pltpu.make_async_copy(wv_hbm.at[:, cols], vbuf.at[h, ROWS : 2 * ROWS], load_sem.at[h, 4]),
        )

    @pl.loop(0, NH)
    def _(h):
        for copy in loads(h):
            copy.start()

    w_copy = pltpu.make_async_copy(w_hbm, wbuf, w_sem)

    barrier = pltpu.get_barrier_semaphore()
    for peer in (x_up, x_down, y_up, y_down, flip):
        pl.semaphore_signal(barrier, inc=1, device_id={"tm": peer}, device_id_type=MESH)
    pl.semaphore_signal(barrier, inc=1, device_id={"head": other}, device_id_type=MESH)

    @pl.when(zl > 0)
    def _():
        pl.semaphore_signal(barrier, inc=1, device_id={"head": hd - 2}, device_id_type=MESH)

    @pl.when(zl < HEADS_Z - 1)
    def _():
        pl.semaphore_signal(barrier, inc=1, device_id={"head": hd + 2}, device_id_type=MESH)

    @pl.when((zl > 0) & (zl < HEADS_Z - 1))
    def _():
        pl.semaphore_wait(barrier, 8)

    @pl.when((zl == 0) | (zl == HEADS_Z - 1))
    def _():
        pl.semaphore_wait(barrier, 7)

    def kslot(buf, h, slot):
        return buf.at[h, slot * 2 * ROWS : (slot + 1) * 2 * ROWS]

    def chunk(h, index):
        return qbuf.at[h, index * ROWS : (index + 1) * ROWS]

    def kv_copies(h):
        up = kv_peer(h % 2, True)
        down = kv_peer(h % 2, False)
        return Plan(
            (kslot(kbuf, h, 0), kslot(kbuf, h, 1), kv_send.at[h, 0], kv_recv.at[h, 0, 0], up),
            (kslot(vbuf, h, 0), kslot(vbuf, h, 3), kv_send.at[h, 3], kv_recv.at[h, 1, 2], down),
            (kslot(vbuf, h, 0), kslot(vbuf, h, 1), kv_send.at[h, 1], kv_recv.at[h, 1, 0], up),
            (kslot(kbuf, h, 0), kslot(kbuf, h, 3), kv_send.at[h, 2], kv_recv.at[h, 0, 2], down),
            (kslot(kbuf, h, 1), kslot(kbuf, h, 2), kv_send.at[h, 4], kv_recv.at[h, 0, 1], up),
            (kslot(vbuf, h, 3), kslot(vbuf, h, 2), kv_send.at[h, 5], kv_recv.at[h, 1, 1], down),
        )

    def q_copies(h):
        up = q_peer(h % 2, True)
        down = q_peer(h % 2, False)
        return Plan(
            (chunk(h, 0), chunk(h, 1), q_send.at[h, 0], q_recv.at[h, 1], flip),
            (chunk(h, 0), chunk(h, 2), q_send.at[h, 1], q_recv.at[h, 2], up),
            (chunk(h, 0), chunk(h, 6), q_send.at[h, 2], q_recv.at[h, 6], down),
            (chunk(h, 1), chunk(h, 7), q_send.at[h, 4], q_recv.at[h, 7], down),
            (chunk(h, 1), chunk(h, 3), q_send.at[h, 3], q_recv.at[h, 3], up),
            (chunk(h, 2), chunk(h, 4), q_send.at[h, 5], q_recv.at[h, 4], up),
            (chunk(h, 7), chunk(h, 5), q_send.at[h, 6], q_recv.at[h, 5], down),
        )

    def o_copies(h):
        up = q_peer(h % 2, True)
        down = q_peer(h % 2, False)

        def one(src, dst, index, peer):
            return (pbuf.at[h, src], ibuf.at[h, dst], o_send.at[h, index], o_recv.at[h, dst], peer)

        return Plan(
            one(4, 0, 0, down),
            one(5, 1, 1, up),
            one(3, 3, 2, down),
            one(6, 4, 3, up),
            one(2, 2, 4, down),
            one(7, 5, 5, up),
            one(1, 6, 6, flip),
        )

    def first(h):
        for copy in loads(h):
            copy.wait()
        q = q_copies(h)
        kv = kv_copies(h)
        for plan, indices in ((q, (0, 1, 2)), (kv, (0, 1, 2, 3))):
            for index in indices:
                plan[index].start()

    def second(h):
        q = q_copies(h)
        kv = kv_copies(h)
        q[0].wait_recv()
        q[3].start()
        q[4].start()
        q[1].wait_recv()
        q[5].start()
        kv[0].wait_recv()
        kv[4].start()
        kv[1].wait_recv()
        kv[5].start()

    def third(h):
        q = q_copies(h)
        q[3].wait_recv()
        q[6].start()

    def attention(h):
        par = h % 2
        q = q_copies(h)
        kv = kv_copies(h)
        for plan, indices in ((q, (2, 4, 5, 6)), (kv, (2, 3, 4, 5))):
            for index in indices:
                plan[index].wait_recv()
        vt[0:HD, :] = vbuf[h].T
        o = o_copies(h)

        @pl.loop(0, RING)
        def _(step):
            place = (step + 2) % 4
            queries = qbuf[h, pl.ds(pl.multiple_of(place * 2 * ROWS, 2 * ROWS), 2 * ROWS), :]
            scores = dot_nt(kbuf[h], queries).reshape(KB, BLOCK, 2 * ROWS)
            hidden = pen[par, place]
            tops = jnp.max(scores, axis=1) * LOG2 - hidden
            peak = jnp.maximum(jnp.max(tops, axis=0, keepdims=True), FLOOR)
            peak = peak.astype(jnp.bfloat16).astype(jnp.float32)
            shift = peak + hidden
            weights = jnp.exp2(scores * LOG2 - shift[:, None, :]).astype(jnp.bfloat16)
            result = jnp.dot(
                vt[...], weights.reshape(KEYS, 2 * ROWS), preferred_element_type=jnp.float32
            )
            numer = result[0:HD, :].astype(jnp.bfloat16)
            stats = stat_rows(peak, result[HD : HD + 1, :])
            for half in range(2):
                lanes = slice(half * ROWS, (half + 1) * ROWS)
                pbuf[h, place * 2 + half, 0:HD, :] = numer[:, lanes]
                pbuf[h, place * 2 + half, HD:MSG, :] = stats[:, lanes]

            @pl.when(step == 0)
            def _():
                o[0].start()
                o[1].start()

            @pl.when(step == 1)
            def _():
                o[3].start()

        o[2].start()

    def fold(h):
        o = o_copies(h)
        for source, mine, nxt in ((0, 2, 4), (1, 7, 5)):
            o[source].wait_recv()
            numer, peak, total = merge([unpack(pbuf[h, mine]), unpack(ibuf[h, source])])
            pbuf[h, mine, 0:HD, :] = numer.astype(jnp.bfloat16)
            pbuf[h, mine, HD:MSG, :] = stat_rows(peak, total)
            o[nxt].start()

    def cross(h):
        o = o_copies(h)
        o[2].wait_recv()
        o[5].wait_recv()
        numer, peak, total = merge([unpack(pbuf[h, 1]), unpack(ibuf[h, 3]), unpack(ibuf[h, 5])])
        pbuf[h, 1, 0:HD, :] = numer.astype(jnp.bfloat16)
        pbuf[h, 1, HD:MSG, :] = stat_rows(peak, total)
        o[6].start()

    def finish(h):
        o = o_copies(h)
        o[3].wait_recv()
        o[4].wait_recv()
        o[6].wait_recv()
        numer, peak, total = merge(
            [unpack(pbuf[h, 0]), unpack(ibuf[h, 2]), unpack(ibuf[h, 4]), unpack(ibuf[h, 6])]
        )
        att[:, pl.ds(pl.multiple_of(h * HD, HD), HD)] = (numer / total).T.astype(jnp.bfloat16)

    def prepare():
        vt[HD:MSG, :] = jnp.ones((MSG - HD, KEYS), jnp.bfloat16)
        groups = sees_ref.shape[0]
        table = (
            (lax.broadcasted_iota(jnp.int32, (groups, NBLK), 0) == group_ref[...])
            .astype(jnp.float32)
            .astype(jnp.bfloat16)
        )
        allowed = sees_ref[...].astype(jnp.float32).astype(jnp.bfloat16)
        for par in range(2):
            row = lax.broadcasted_iota(jnp.int32, (KB, NBLK), 0)
            slot = row // 4
            if par == 0:
                source = y * 8 + s * 4 + (x + 4 - slot) % 4
            else:
                source = ((y + 4 - slot) % 4) * 8 + s * 4 + x
            key_block = source * 2 + row % 2 + ((row // 2) % 2) * (NBLK // 2)
            picks = (
                (lax.broadcasted_iota(jnp.int32, (KB, NBLK), 1) == key_block)
                .astype(jnp.float32)
                .astype(jnp.bfloat16)
            )
            key_group = dot_nt(picks, table).astype(jnp.bfloat16)
            seen_by = dot_nt(key_group, allowed).astype(jnp.bfloat16)
            for place in range(RING):
                lane = lax.broadcasted_iota(jnp.int32, (NBLK, 2 * ROWS), 1)
                half = lane // ROWS
                side = s + half - 2 * s * half
                if par == 0:
                    origin = ((y + 4 - place) % 4) * 8 + side * 4 + x
                else:
                    origin = y * 8 + side * 4 + (x + 4 - place) % 4
                query_block = NBLK // 2 + origin * 2 + (lane // BLOCK) % 2
                wanted = (
                    (lax.broadcasted_iota(jnp.int32, (NBLK, 2 * ROWS), 0) == query_block)
                    .astype(jnp.float32)
                    .astype(jnp.bfloat16)
                )
                query_group = jnp.dot(table, wanted, preferred_element_type=jnp.float32).astype(
                    jnp.bfloat16
                )
                visible = jnp.dot(seen_by, query_group, preferred_element_type=jnp.float32)
                pen[par, place] = jnp.where(visible > 0.5, 0.0, BIG)

    stages = ((first, 0), (second, 1), (third, 2), (attention, 3), (fold, 4), (cross, 5), (finish, 6))

    @pl.loop(0, NH + 6)
    def _(it):
        for stage, lag in stages:
            @pl.when((it >= lag) & (it < NH + lag))
            def _():
                stage(it - lag)

            if lag == 0:
                @pl.when(it == 0)
                def _():
                    prepare()
                    w_copy.start()

    w_copy.wait()

    def pair_copy(q):
        return remote(pst.at[q], pin.at[q], p_send.at[q], p_recv.at[q], head=other)

    def rows_of(sub):
        return pl.ds(sub * SUBR, SUBR)

    def right_copy(q, sub):
        r = rows_of(sub)
        return remote(rst.at[q, r], rin.at[0, q, r], r_send.at[q, sub], r_recv.at[0, q, sub], head=hd + 2)

    def left_copy(q, sub):
        r = rows_of(sub)
        return remote(rst.at[q, r], rin.at[1, q, r], r_send.at[q, sub], r_recv.at[1, q, sub], head=hd - 2)

    def project(block):
        cols = pl.ds(pl.multiple_of(block * FEAT, FEAT), FEAT)
        return jnp.dot(att[...], wbuf[:, cols], preferred_element_type=jnp.float32)

    def order(j):
        low = (zl < 2).astype(jnp.int32)
        return j + (HEADS_Z - 1 - 2 * j) * low

    @pl.loop(0, HEADS_Z)
    def _(j):
        q = order(j)
        pst[q] = project(2 * q + 1 - core).astype(jnp.bfloat16)
        pair_copy(q).start()

    @pl.loop(0, HEADS_Z)
    def _(j):
        q = order(j)
        mine = project(2 * q + core)
        pair_copy(q).wait_recv()
        own[q] = mine + pin[q].astype(jnp.float32)

        for sub in range(SUB):
            r = rows_of(sub)

            @pl.when(q > zl)
            def _():
                @pl.when(zl > 0)
                def _():
                    right_copy(q, sub).wait_recv()
                    rst[q, r] = (own[q, r] + rin[0, q, r].astype(jnp.float32)).astype(jnp.bfloat16)

                @pl.when(zl == 0)
                def _():
                    rst[q, r] = own[q, r].astype(jnp.bfloat16)

                right_copy(q, sub).start()

            @pl.when(q < zl)
            def _():
                @pl.when(zl < HEADS_Z - 1)
                def _():
                    left_copy(q, sub).wait_recv()
                    rst[q, r] = (own[q, r] + rin[1, q, r].astype(jnp.float32)).astype(jnp.bfloat16)

                @pl.when(zl == HEADS_Z - 1)
                def _():
                    rst[q, r] = own[q, r].astype(jnp.bfloat16)

                left_copy(q, sub).start()

    for sub in range(SUB):
        r = rows_of(sub)

        @pl.when(zl > 0)
        def _():
            right_copy(zl, sub).wait_recv()
            own[zl, r] = own[zl, r] + rin[0, zl, r].astype(jnp.float32)

        @pl.when(zl < HEADS_Z - 1)
        def _():
            left_copy(zl, sub).wait_recv()
            own[zl, r] = own[zl, r] + rin[1, zl, r].astype(jnp.float32)

        out_ref[r, :] = (own[zl, r] * gate_ref[...]).astype(jnp.bfloat16)

    @pl.loop(0, NH)
    def _(h):
        for plan in (kv_copies(h), q_copies(h), o_copies(h)):
            for index in range(len(plan)):
                plan[index].wait_send()

    @pl.loop(0, HEADS_Z)
    def _(q):
        pair_copy(q).wait_send()
        for sub in range(SUB):
            @pl.when(q > zl)
            def _():
                right_copy(q, sub).wait_send()

            @pl.when(q < zl)
            def _():
                left_copy(q, sub).wait_send()


def body(
    queries,
    window_keys,
    window_values,
    context_keys,
    context_values,
    block_group,
    sees,
    out_weight,
    gate,
):
    hbm = pl.BlockSpec(memory_space=pl.ANY)
    vmem = pl.BlockSpec(memory_space=pltpu.VMEM)
    dma = pltpu.SemaphoreType.DMA
    width = out_weight.shape[1]
    bf16 = jnp.bfloat16
    return pl.pallas_call(
        kernel,
        out_shape=jax.ShapeDtypeStruct((ROWS, FEAT), bf16),
        in_specs=[hbm] * 5 + [vmem, vmem, hbm, vmem],
        out_specs=vmem,
        scratch_shapes=[
            pltpu.VMEM((NH, QCH * ROWS, HD), bf16),
            pltpu.VMEM((NH, KEYS, HD), bf16),
            pltpu.VMEM((NH, KEYS, HD), bf16),
            pltpu.VMEM((MSG, KEYS), bf16),
            pltpu.VMEM((2, RING, KB, 2 * ROWS), jnp.float32),
            pltpu.VMEM((NH, QCH, MSG, HD), bf16),
            pltpu.VMEM((NH, 7, MSG, HD), bf16),
            pltpu.VMEM((ROWS, FEAT), bf16),
            pltpu.VMEM((FEAT, width), bf16),
            pltpu.VMEM((HEADS_Z, ROWS, FEAT), bf16),
            pltpu.VMEM((HEADS_Z, ROWS, FEAT), bf16),
            pltpu.VMEM((HEADS_Z, ROWS, FEAT), jnp.float32),
            pltpu.VMEM((HEADS_Z, ROWS, FEAT), bf16),
            pltpu.VMEM((2, HEADS_Z, ROWS, FEAT), bf16),
            dma((NH, 5)),
            dma(()),
            dma((NH, 6)),
            dma((NH, 2, 3)),
            dma((NH, 7)),
            dma((NH, 8)),
            dma((NH, 7)),
            dma((NH, 7)),
            dma((HEADS_Z,)),
            dma((HEADS_Z,)),
            dma((HEADS_Z, SUB)),
            dma((2, HEADS_Z, SUB)),
        ],
        compiler_params=pltpu.CompilerParams(
            collective_id=0, has_side_effects=True, vmem_limit_bytes=56 * 1024 * 1024
        ),
    )(
        queries,
        window_keys,
        window_values,
        context_keys,
        context_values,
        block_group.reshape(1, NBLK),
        sees,
        out_weight,
        gate.reshape(1, FEAT),
    )


def solution(mesh):
    placed = (
        P("tm", "head"),
        P("tm", "head"),
        P("tm", "head"),
        P("tm", "head"),
        P("tm", "head"),
        P(),
        P(),
        P("head", None),
        P("head"),
    )
    return jax.shard_map(
        body, mesh=mesh, in_specs=placed, out_specs=P("tm", "head"), check_vma=False
    )
```

```python
import functools
import math

import jax
import jax.numpy as jnp
from jax import lax
from jax.experimental import pallas as pl
from jax.experimental.pallas import tpu as pltpu
from jax.sharding import PartitionSpec as P

HD = 128
BLOCK = 64
ROWS = 128
NH = 6
FEAT = NH * HD
RING = 4
KEYS = 2 * ROWS * RING
KB = KEYS // BLOCK
QCH = 2 * RING
MSG = HD + 16
HEADS_Z = 4
NBLK = 128
SUB = 2
EARLY = 4
TURN = 3
SUBR = ROWS // SUB
BIG = 1e30
FLOOR = -1e29
MESH = pl.DeviceIdType.MESH
LOG2 = math.log2(math.e) / math.sqrt(HD)


def remote(src, dst, send, recv, **device):
    return pltpu.make_async_remote_copy(
        src_ref=src, dst_ref=dst, send_sem=send, recv_sem=recv, device_id=device, device_id_type=MESH
    )


class Plan:
    def __init__(self, *entries):
        self.entries = entries

    def __getitem__(self, index):
        src, dst, send, recv, peer = self.entries[index]
        return remote(src, dst, send, recv, tm=peer)

    def __len__(self):
        return len(self.entries)


def dot_nt(a, b):
    return lax.dot_general(a, b, (((1,), (1,)), ((), ())), preferred_element_type=jnp.float32)


def unpack(message):
    stats = message[HD:MSG, :].astype(jnp.float32)
    return (message[0:HD, :].astype(jnp.float32), stats[0:1, :], stats[1:2, :] + stats[2:3, :])


def merge(parts):
    peak = parts[0][1]
    for part in parts[1:]:
        peak = jnp.maximum(peak, part[1])
    numer = None
    total = None
    for part in parts:
        factor = jnp.exp2(part[1] - peak)
        numer = part[0] * factor if numer is None else numer + part[0] * factor
        total = part[2] * factor if total is None else total + part[2] * factor
    return (numer, peak, total)


def stat_rows(peak, total):
    high = total.astype(jnp.bfloat16).astype(jnp.float32)
    rows = lax.broadcasted_iota(jnp.int32, (MSG - HD, peak.shape[1]), 0)
    picked = jnp.where(rows == 0, peak, jnp.where(rows == 1, high, total - high))
    return picked.astype(jnp.bfloat16)


def kernel(
    q_hbm,
    wk_hbm,
    wv_hbm,
    ck_hbm,
    cv_hbm,
    group_ref,
    sees_ref,
    w_hbm,
    gate_ref,
    out_ref,
    qbuf,
    kbuf,
    vbuf,
    vt,
    pen,
    pbuf,
    ibuf,
    att,
    wbuf,
    sa,
    sb,
    acc,
    pst,
    pin,
    own,
    rst,
    rin,
    load_sem,
    w_sem,
    kv_send,
    kv_recv,
    q_send,
    q_recv,
    o_send,
    o_recv,
    p_send,
    p_recv,
    r_send,
    r_recv,
):
    t = lax.axis_index("tm")
    hd = lax.axis_index("head")
    x = t % 4
    s = (t // 4) % 2
    y = t // 8
    zl = hd // 2
    core = hd % 2
    flip = t + 4 - 8 * s
    other = hd + 1 - 2 * core

    def along(delta):
        return (t - x + (x + delta + 4) % 4, t + ((y + delta + 4) % 4 - y) * 8)

    x_up, y_up = along(1)
    x_down, y_down = along(-1)

    def kv_peer(par, up):
        a, b = (x_up, y_up) if up else (x_down, y_down)
        return a * (1 - par) + b * par

    def far_peer(par):
        a, b = along(2)
        return a * par + b * (1 - par)

    def q_peer(par, up):
        a, b = (x_up, y_up) if up else (x_down, y_down)
        return a * par + b * (1 - par)

    def loads(h):
        cols = pl.ds(pl.multiple_of(h * HD, HD), HD)
        return (
            pltpu.make_async_copy(q_hbm.at[:, cols], qbuf.at[h, 0:ROWS], load_sem.at[h, 0]),
            pltpu.make_async_copy(ck_hbm.at[:, cols], kbuf.at[h, 0:ROWS], load_sem.at[h, 1]),
            pltpu.make_async_copy(wk_hbm.at[:, cols], kbuf.at[h, ROWS : 2 * ROWS], load_sem.at[h, 2]),
            pltpu.make_async_copy(cv_hbm.at[:, cols], vbuf.at[h, 0:ROWS], load_sem.at[h, 3]),
            pltpu.make_async_copy(wv_hbm.at[:, cols], vbuf.at[h, ROWS : 2 * ROWS], load_sem.at[h, 4]),
        )

    @pl.loop(0, NH)
    def _(h):
        for copy in loads(h):
            copy.start()

    w_copy = pltpu.make_async_copy(w_hbm, wbuf, w_sem)

    barrier = pltpu.get_barrier_semaphore()
    x_far, y_far = along(2)
    for peer in (x_up, x_down, y_up, y_down, flip, x_far, y_far):
        pl.semaphore_signal(barrier, inc=1, device_id={"tm": peer}, device_id_type=MESH)
    pl.semaphore_signal(barrier, inc=1, device_id={"head": other}, device_id_type=MESH)

    @pl.when(zl > 0)
    def _():
        pl.semaphore_signal(barrier, inc=1, device_id={"head": hd - 2}, device_id_type=MESH)

    @pl.when(zl < HEADS_Z - 1)
    def _():
        pl.semaphore_signal(barrier, inc=1, device_id={"head": hd + 2}, device_id_type=MESH)

    @pl.when((zl > 0) & (zl < HEADS_Z - 1))
    def _():
        pl.semaphore_wait(barrier, 10)

    @pl.when((zl == 0) | (zl == HEADS_Z - 1))
    def _():
        pl.semaphore_wait(barrier, 9)

    def kslot(buf, h, slot):
        return buf.at[h, slot * 2 * ROWS : (slot + 1) * 2 * ROWS]

    def chunk(h, index):
        return qbuf.at[h, index * ROWS : (index + 1) * ROWS]

    def kv_copies(h):
        up = kv_peer(h % 2, True)
        down = kv_peer(h % 2, False)
        return Plan(
            (kslot(kbuf, h, 0), kslot(kbuf, h, 1), kv_send.at[h, 0], kv_recv.at[h, 0, 0], up),
            (kslot(vbuf, h, 0), kslot(vbuf, h, 3), kv_send.at[h, 3], kv_recv.at[h, 1, 2], down),
            (kslot(vbuf, h, 0), kslot(vbuf, h, 1), kv_send.at[h, 1], kv_recv.at[h, 1, 0], up),
            (kslot(kbuf, h, 0), kslot(kbuf, h, 3), kv_send.at[h, 2], kv_recv.at[h, 0, 2], down),
            (kslot(kbuf, h, 1), kslot(kbuf, h, 2), kv_send.at[h, 4], kv_recv.at[h, 0, 1], up),
            (kslot(vbuf, h, 3), kslot(vbuf, h, 2), kv_send.at[h, 5], kv_recv.at[h, 1, 1], down),
        )

    def q_copies(h):
        up = q_peer(h % 2, True)
        down = q_peer(h % 2, False)

        def one(src, dst, index, peer):
            return (chunk(h, src), chunk(h, dst), q_send.at[h, index], q_recv.at[h, dst], peer)

        return Plan(
            one(0, 4, 0, flip),
            one(0, 1, 1, up),
            one(0, 3, 2, down),
            one(4, 7, 3, down),
            one(4, 5, 4, up),
            one(1, 2, 5, up),
            one(7, 6, 6, down),
        )

    def o_copy(h, side, place):
        peer = (q_peer(h % 2, False), far_peer(h % 2), q_peer(h % 2, True))[place - 1]
        slot = side * 3 + place - 1
        return remote(
            pbuf.at[h, side * RING + place], ibuf.at[h, slot], o_send.at[h, slot], o_recv.at[h, slot], tm=peer
        )

    def o_flip(h):
        return remote(pbuf.at[h, RING], ibuf.at[h, 6], o_send.at[h, 6], o_recv.at[h, 6], tm=flip)

    def first(h):
        for copy in loads(h):
            copy.wait()
        q = q_copies(h)
        kv = kv_copies(h)
        for plan, indices in ((q, (0, 1, 2)), (kv, (0, 1, 2, 3))):
            for index in indices:
                plan[index].start()

    def second(h):
        q = q_copies(h)
        kv = kv_copies(h)
        kv[0].wait_recv()
        kv[4].start()
        kv[1].wait_recv()
        kv[5].start()
        q[1].wait_recv()
        q[5].start()
        q[0].wait_recv()
        q[3].start()
        q[4].start()

    def third(h):
        q = q_copies(h)
        q[3].wait_recv()
        q[6].start()

    def attention(h):
        par = h % 2
        q = q_copies(h)
        kv = kv_copies(h)
        late = (h >= TURN).astype(jnp.int32)

        def arrived(plan, indices):
            for index in indices:
                plan[index].wait_recv()

        def score(index, dest):
            block = (index + 2 * late) % 4
            queries = qbuf[h, pl.ds(pl.multiple_of(block * 2 * ROWS, 2 * ROWS), 2 * ROWS), :]
            dest[...] = dot_nt(kbuf[h], queries)

        def weigh(index, source):
            block = (index + 2 * late) % 4
            scores = source[...].reshape(KB, BLOCK, 2 * ROWS)
            hidden = pen[par, block]
            tops = jnp.max(scores, axis=1) * LOG2 - hidden
            peak = jnp.maximum(jnp.max(tops, axis=0, keepdims=True), FLOOR)
            peak = peak.astype(jnp.bfloat16).astype(jnp.float32)
            shift = peak + hidden
            weights = jnp.exp2(scores * LOG2 - shift[:, None, :]).astype(jnp.bfloat16)
            result = jnp.dot(
                vt[...], weights.reshape(KEYS, 2 * ROWS), preferred_element_type=jnp.float32
            )
            numer = result[0:HD, :].astype(jnp.bfloat16)
            stats = stat_rows(peak, result[HD : HD + 1, :])
            for half in range(2):
                lanes = slice(half * ROWS, (half + 1) * ROWS)
                pbuf[h, block * 2 + half, 0:HD, :] = numer[:, lanes]
                pbuf[h, block * 2 + half, HD:MSG, :] = stats[:, lanes]

        arrived(kv, (2, 3, 4, 5))
        arrived(q, (2, 5))

        @pl.when(late == 1)
        def _():
            arrived(q, (4, 6))

        vt[0:HD, :] = vbuf[h].T
        score(0, sa)
        score(1, sb)
        weigh(0, sa)

        @pl.when(late == 0)
        def _():
            arrived(q, (4, 6))

        score(2, sa)
        weigh(1, sb)
        for place in (2, 3, 1):
            o_copy(h, late, place).start()
        score(3, sb)
        weigh(2, sa)
        weigh(3, sb)
        for place in (2, 3, 1):
            o_copy(h, 1 - late, place).start()

    def put(h, index, parts):
        numer, peak, total = merge(parts)
        pbuf[h, index, 0:HD, :] = numer.astype(jnp.bfloat16)
        pbuf[h, index, HD:MSG, :] = stat_rows(peak, total)

    def take(h, indices):
        return [unpack(ibuf[h, index]) for index in indices]

    def fold(h):
        o = o_copies(h)

        @pl.when(h < DIRECT)
        def _():
            for source, mine, nxt in ((0, 2, 4), (1, 7, 5)):
                o[source].wait_recv()
                put(h, mine, [unpack(pbuf[h, mine])] + take(h, (source,)))
                o[nxt].start()

    def cross(h):
        for place in (1, 2, 3):
            o_copy(h, 1, place).wait_recv()
        put(h, RING, [unpack(pbuf[h, RING])] + take(h, (3, 4, 5)))
        o_flip(h).start()

    def finish(h):
        for place in (1, 2, 3):
            o_copy(h, 0, place).wait_recv()
        o_flip(h).wait_recv()
        numer, peak, total = merge([unpack(pbuf[h, 0])] + take(h, (0, 1, 2, 6)))
        att[:, pl.ds(pl.multiple_of(h * HD, HD), HD)] = (numer / total).T.astype(jnp.bfloat16)

    def prepare():
        vt[HD:MSG, :] = jnp.ones((MSG - HD, KEYS), jnp.bfloat16)
        groups = sees_ref.shape[0]
        table = (
            (lax.broadcasted_iota(jnp.int32, (groups, NBLK), 0) == group_ref[...].reshape(1, NBLK))
            .astype(jnp.float32)
            .astype(jnp.bfloat16)
        )
        allowed = sees_ref[...].astype(jnp.float32).astype(jnp.bfloat16)
        for par in range(2):
            row = lax.broadcasted_iota(jnp.int32, (KB, NBLK), 0)
            slot = row // 4
            if par == 0:
                source = y * 8 + s * 4 + (x + 4 - slot) % 4
            else:
                source = ((y + 4 - slot) % 4) * 8 + s * 4 + x
            key_block = source * 2 + row % 2 + ((row // 2) % 2) * (NBLK // 2)
            picks = (
                (lax.broadcasted_iota(jnp.int32, (KB, NBLK), 1) == key_block)
                .astype(jnp.float32)
                .astype(jnp.bfloat16)
            )
            key_group = dot_nt(picks, table).astype(jnp.bfloat16)
            seen_by = dot_nt(key_group, allowed).astype(jnp.bfloat16)
            for place in range(RING):
                lane = lax.broadcasted_iota(jnp.int32, (NBLK, 2 * ROWS), 1)
                shift = 2 * (place % 2) + lane // ROWS
                side = 1 - s if place >= 2 else s
                if par == 0:
                    origin = ((y + 4 - shift) % 4) * 8 + side * 4 + x
                else:
                    origin = y * 8 + side * 4 + (x + 4 - shift) % 4
                query_block = NBLK // 2 + origin * 2 + (lane // BLOCK) % 2
                wanted = (
                    (lax.broadcasted_iota(jnp.int32, (NBLK, 2 * ROWS), 0) == query_block)
                    .astype(jnp.float32)
                    .astype(jnp.bfloat16)
                )
                query_group = jnp.dot(table, wanted, preferred_element_type=jnp.float32).astype(
                    jnp.bfloat16
                )
                visible = jnp.dot(seen_by, query_group, preferred_element_type=jnp.float32)
                pen[par, place] = jnp.where(visible > 0.5, 0.0, BIG)

    first(0)
    first(1)
    prepare()
    w_copy.start()
    second(0)
    first(2)
    second(1)
    third(0)

    def project(block, low, high):
        cols = pl.ds(pl.multiple_of(block * FEAT, FEAT), FEAT)
        rows = slice(low * HD, high * HD)
        return jnp.dot(att[:, rows], wbuf[rows, cols], preferred_element_type=jnp.float32)

    def begin(low, high):
        @pl.loop(low, high)
        def _(block):
            acc[block] = project(block, 0, EARLY)

    def start_projection(h):
        w_copy.wait()
        begin(0, HEADS_Z)

    def go_on_projection(h):
        begin(HEADS_Z, 2 * HEADS_Z)

    stages = (
        (attention, 0, 0, NH),
        (third, -1, 1, NH),
        (start_projection, 1, NH - 1, NH),
        (cross, 1, 0, NH),
        (finish, 2, 0, NH),
        (go_on_projection, 2, NH - 2, NH - 1),
        (first, -3, 3, NH),
        (second, -2, 2, NH),
    )

    @pl.loop(0, NH + 2)
    def _(it):
        for stage, lag, low, high in stages:
            @pl.when((it >= lag + low) & (it < high + lag))
            def _():
                stage(it - lag)

    def pair_copy(q):
        return remote(pst.at[q], pin.at[q], p_send.at[q], p_recv.at[q], head=other)

    def rows_of(sub):
        return pl.ds(sub * SUBR, SUBR)

    def right_copy(q, sub):
        r = rows_of(sub)
        return remote(rst.at[q, r], rin.at[0, q, r], r_send.at[q, sub], r_recv.at[0, q, sub], head=hd + 2)

    def left_copy(q, sub):
        r = rows_of(sub)
        return remote(rst.at[q, r], rin.at[1, q, r], r_send.at[q, sub], r_recv.at[1, q, sub], head=hd - 2)

    def order(j):
        low = (zl < 2).astype(jnp.int32)
        return j + (HEADS_Z - 1 - 2 * j) * low

    def theirs(q):
        pst[q] = (acc[2 * q + 1 - core] + project(2 * q + 1 - core, EARLY, NH)).astype(jnp.bfloat16)
        pair_copy(q).start()

    theirs(order(0))
    theirs(order(1))

    @pl.loop(0, HEADS_Z)
    def _(j):
        q = order(j)
        mine = acc[2 * q + core] + project(2 * q + core, EARLY, NH)
        pair_copy(q).wait_recv()
        mine = mine + pin[q].astype(jnp.float32)
        own[q] = mine
        for edge, sends in ((0, right_copy), (HEADS_Z - 1, left_copy)):
            @pl.when((zl == edge) & (q != zl))
            def _():
                rst[q] = mine.astype(jnp.bfloat16)
                for sub in range(SUB):
                    sends(q, sub).start()

        @pl.when(j < 2)
        def _():
            theirs(order(j + 2))

    def relay(side, copies, q, sub):
        r = rows_of(sub)
        copies(q, sub).wait_recv()
        rst[q, r] = (own[q, r] + rin[side, q, r].astype(jnp.float32)).astype(jnp.bfloat16)
        copies(q, sub).start()

    for place in range(1, HEADS_Z - 1):
        near, far = ((0, right_copy), (1, left_copy)) if place == 1 else ((1, left_copy), (0, right_copy))
        ends = (3, 0) if place == 1 else (0, 3)

        @pl.when(zl == place)
        def _():
            for sub in range(SUB):
                relay(*near, ends[0], sub)
            for sub in range(SUB):
                relay(*far, ends[1], sub)
                relay(*near, HEADS_Z - 1 - place, sub)

    for sub in range(SUB):
        r = rows_of(sub)

        @pl.when(zl > 0)
        def _():
            right_copy(zl, sub).wait_recv()
            own[zl, r] = own[zl, r] + rin[0, zl, r].astype(jnp.float32)

        @pl.when(zl < HEADS_Z - 1)
        def _():
            left_copy(zl, sub).wait_recv()
            own[zl, r] = own[zl, r] + rin[1, zl, r].astype(jnp.float32)

        out_ref[r, :] = (own[zl, r] * gate_ref[...].reshape(1, FEAT)).astype(jnp.bfloat16)

    @pl.loop(0, NH)
    def _(h):
        for plan in (kv_copies(h), q_copies(h)):
            for index in range(len(plan)):
                plan[index].wait_send()
        for side in range(2):
            for place in (1, 2, 3):
                o_copy(h, side, place).wait_send()
        o_flip(h).wait_send()

    @pl.loop(0, HEADS_Z)
    def _(q):
        pair_copy(q).wait_send()
        for sub in range(SUB):
            @pl.when(q > zl)
            def _():
                right_copy(q, sub).wait_send()

            @pl.when(q < zl)
            def _():
                left_copy(q, sub).wait_send()


def body(
    queries,
    window_keys,
    window_values,
    context_keys,
    context_values,
    block_group,
    sees,
    out_weight,
    gate,
):
    hbm = pl.BlockSpec(memory_space=pl.ANY)
    vmem = pl.BlockSpec(memory_space=pltpu.VMEM)
    dma = pltpu.SemaphoreType.DMA
    width = out_weight.shape[1]
    bf16 = jnp.bfloat16
    return pl.pallas_call(
        kernel,
        out_shape=jax.ShapeDtypeStruct((ROWS, FEAT), bf16),
        in_specs=[hbm] * 5 + [vmem, vmem, hbm, vmem],
        out_specs=vmem,
        scratch_shapes=[
            pltpu.VMEM((NH, QCH * ROWS, HD), bf16),
            pltpu.VMEM((NH, KEYS, HD), bf16),
            pltpu.VMEM((NH, KEYS, HD), bf16),
            pltpu.VMEM((MSG, KEYS), bf16),
            pltpu.VMEM((2, RING, KB, 2 * ROWS), jnp.float32),
            pltpu.VMEM((NH, QCH, MSG, HD), bf16),
            pltpu.VMEM((NH, 7, MSG, HD), bf16),
            pltpu.VMEM((ROWS, FEAT), bf16),
            pltpu.VMEM((FEAT, width), bf16),
            pltpu.VMEM((KEYS, 2 * ROWS), jnp.float32),
            pltpu.VMEM((KEYS, 2 * ROWS), jnp.float32),
            pltpu.VMEM((2 * HEADS_Z, ROWS, FEAT), jnp.float32),
            pltpu.VMEM((HEADS_Z, ROWS, FEAT), bf16),
            pltpu.VMEM((HEADS_Z, ROWS, FEAT), bf16),
            pltpu.VMEM((HEADS_Z, ROWS, FEAT), jnp.float32),
            pltpu.VMEM((HEADS_Z, ROWS, FEAT), bf16),
            pltpu.VMEM((2, HEADS_Z, ROWS, FEAT), bf16),
            dma((NH, 5)),
            dma(()),
            dma((NH, 6)),
            dma((NH, 2, 3)),
            dma((NH, 7)),
            dma((NH, 8)),
            dma((NH, 7)),
            dma((NH, 7)),
            dma((HEADS_Z,)),
            dma((HEADS_Z,)),
            dma((HEADS_Z, SUB)),
            dma((2, HEADS_Z, SUB)),
        ],
        compiler_params=pltpu.CompilerParams(
            collective_id=0, has_side_effects=True, vmem_limit_bytes=56 * 1024 * 1024
        ),
    )(
        queries,
        window_keys,
        window_values,
        context_keys,
        context_values,
        block_group,
        sees,
        out_weight,
        gate,
    )


def solution(mesh):
    placed = (
        P("tm", "head"),
        P("tm", "head"),
        P("tm", "head"),
        P("tm", "head"),
        P("tm", "head"),
        P(),
        P(),
        P("head", None),
        P("head"),
    )
    return jax.shard_map(
        body, mesh=mesh, in_specs=placed, out_specs=P("tm", "head"), check_vma=False
    )
```

```python
import functools
import math

import jax
import jax.numpy as jnp
from jax import lax
from jax.experimental import pallas as pl
from jax.experimental.pallas import tpu as pltpu
from jax.sharding import PartitionSpec as P

HD = 128
BLOCK = 64
ROWS = 128
NH = 6
FEAT = NH * HD
RING = 4
KEYS = 2 * ROWS * RING
KB = KEYS // BLOCK
QCH = 2 * RING
MSG = HD + 16
HEADS_Z = 4
NBLK = 128
HALF = ROWS // 2
EARLY = 4
TURN = 4
BIG = 1e30
FLOOR = -1e29
MESH = pl.DeviceIdType.MESH
LOG2 = math.log2(math.e) / math.sqrt(HD)


def remote(src, dst, send, recv, **device):
    return pltpu.make_async_remote_copy(
        src_ref=src, dst_ref=dst, send_sem=send, recv_sem=recv, device_id=device, device_id_type=MESH
    )


class Plan:
    def __init__(self, *entries):
        self.entries = entries

    def __getitem__(self, index):
        src, dst, send, recv, peer = self.entries[index]
        return remote(src, dst, send, recv, tm=peer)

    def __len__(self):
        return len(self.entries)


def dot_nt(a, b):
    return lax.dot_general(a, b, (((1,), (1,)), ((), ())), preferred_element_type=jnp.float32)


def unpack(message):
    stats = message[HD:MSG, :].astype(jnp.float32)
    return (message[0:HD, :].astype(jnp.float32), stats[0:1, :], stats[1:2, :] + stats[2:3, :])


def merge(parts):
    peak = parts[0][1]
    for part in parts[1:]:
        peak = jnp.maximum(peak, part[1])
    numer = None
    total = None
    for part in parts:
        factor = jnp.exp2(part[1] - peak)
        numer = part[0] * factor if numer is None else numer + part[0] * factor
        total = part[2] * factor if total is None else total + part[2] * factor
    return (numer, peak, total)


def stat_rows(peak, total):
    high = total.astype(jnp.bfloat16).astype(jnp.float32)
    rows = lax.broadcasted_iota(jnp.int32, (MSG - HD, peak.shape[1]), 0)
    picked = jnp.where(rows == 0, peak, jnp.where(rows == 1, high, total - high))
    return picked.astype(jnp.bfloat16)


def kernel(
    q_hbm,
    wk_hbm,
    wv_hbm,
    ck_hbm,
    cv_hbm,
    group_ref,
    sees_ref,
    w_hbm,
    gate_ref,
    out_ref,
    qbuf,
    kbuf,
    vbuf,
    vt,
    pen,
    pbuf,
    ibuf,
    att,
    wbuf,
    sa,
    sb,
    acc,
    pst,
    pin,
    own,
    rst,
    rin,
    load_sem,
    w_sem,
    kv_send,
    kv_recv,
    q_send,
    q_recv,
    o_send,
    o_recv,
    p_send,
    p_recv,
    r_send,
    r_recv,
):
    t = lax.axis_index("tm")
    hd = lax.axis_index("head")
    x = t % 4
    s = (t // 4) % 2
    y = t // 8
    zl = hd // 2
    core = hd % 2
    flip = t + 4 - 8 * s
    other = hd + 1 - 2 * core
    z = s * HEADS_Z + zl

    def z_device(delta):
        place = (z + delta + 8) % 8
        return {"tm": t + (place // HEADS_Z - s) * 4, "head": (place % HEADS_Z) * 2 + core}

    def z_side(delta):
        return (((z + delta + 8) % 8) // HEADS_Z + s) % 2

    z_up = z_device(1)
    z_down = z_device(-1)

    def along(delta):
        return (t - x + (x + delta + 4) % 4, t + ((y + delta + 4) % 4 - y) * 8)

    x_up, y_up = along(1)
    x_down, y_down = along(-1)

    def kv_peer(par, up):
        a, b = (x_up, y_up) if up else (x_down, y_down)
        return a * (1 - par) + b * par

    def far_peer(par):
        a, b = along(2)
        return a * par + b * (1 - par)

    def q_peer(par, up):
        a, b = (x_up, y_up) if up else (x_down, y_down)
        return a * par + b * (1 - par)

    def loads(h):
        cols = pl.ds(pl.multiple_of(h * HD, HD), HD)
        return (
            pltpu.make_async_copy(q_hbm.at[:, cols], qbuf.at[h, 0:ROWS], load_sem.at[h, 0]),
            pltpu.make_async_copy(ck_hbm.at[:, cols], kbuf.at[h, 0:ROWS], load_sem.at[h, 1]),
            pltpu.make_async_copy(wk_hbm.at[:, cols], kbuf.at[h, ROWS : 2 * ROWS], load_sem.at[h, 2]),
            pltpu.make_async_copy(cv_hbm.at[:, cols], vbuf.at[h, 0:ROWS], load_sem.at[h, 3]),
            pltpu.make_async_copy(wv_hbm.at[:, cols], vbuf.at[h, ROWS : 2 * ROWS], load_sem.at[h, 4]),
        )

    @pl.loop(0, NH)
    def _(h):
        for copy in loads(h):
            copy.start()

    w_copy = pltpu.make_async_copy(w_hbm, wbuf, w_sem)

    barrier = pltpu.get_barrier_semaphore()
    x_far, y_far = along(2)
    for peer in (x_up, x_down, y_up, y_down, flip, x_far, y_far):
        pl.semaphore_signal(barrier, inc=1, device_id={"tm": peer}, device_id_type=MESH)
    pl.semaphore_signal(barrier, inc=1, device_id={"head": other}, device_id_type=MESH)
    for device in (z_up, z_down):
        pl.semaphore_signal(barrier, inc=1, device_id=device, device_id_type=MESH)
    pl.semaphore_wait(barrier, 10)

    def kslot(buf, h, slot):
        return buf.at[h, slot * 2 * ROWS : (slot + 1) * 2 * ROWS]

    def chunk(h, index):
        return qbuf.at[h, index * ROWS : (index + 1) * ROWS]

    def kv_copies(h):
        up = kv_peer(h % 2, True)
        down = kv_peer(h % 2, False)
        return Plan(
            (kslot(kbuf, h, 0), kslot(kbuf, h, 1), kv_send.at[h, 0], kv_recv.at[h, 0, 0], up),
            (kslot(vbuf, h, 0), kslot(vbuf, h, 3), kv_send.at[h, 3], kv_recv.at[h, 1, 2], down),
            (kslot(vbuf, h, 0), kslot(vbuf, h, 1), kv_send.at[h, 1], kv_recv.at[h, 1, 0], up),
            (kslot(kbuf, h, 0), kslot(kbuf, h, 3), kv_send.at[h, 2], kv_recv.at[h, 0, 2], down),
            (kslot(kbuf, h, 1), kslot(kbuf, h, 2), kv_send.at[h, 4], kv_recv.at[h, 0, 1], up),
            (kslot(vbuf, h, 3), kslot(vbuf, h, 2), kv_send.at[h, 5], kv_recv.at[h, 1, 1], down),
        )

    def q_copies(h):
        up = q_peer(h % 2, True)
        down = q_peer(h % 2, False)

        def one(src, dst, index, peer):
            return (chunk(h, src), chunk(h, dst), q_send.at[h, index], q_recv.at[h, dst], peer)

        return Plan(
            one(0, 4, 0, flip),
            one(0, 1, 1, up),
            one(0, 3, 2, down),
            one(4, 7, 3, down),
            one(4, 5, 4, up),
            one(1, 2, 5, up),
            one(7, 6, 6, down),
        )

    def o_copy(h, side, place):
        peer = (q_peer(h % 2, False), far_peer(h % 2), q_peer(h % 2, True))[place - 1]
        slot = side * 3 + place - 1
        return remote(
            pbuf.at[h, side * RING + place], ibuf.at[h, slot], o_send.at[h, slot], o_recv.at[h, slot], tm=peer
        )

    def o_flip(h, side):
        return remote(
            pbuf.at[h, RING * side],
            ibuf.at[h, 7 - side],
            o_send.at[h, 7 - side],
            o_recv.at[h, 7 - side],
            tm=flip,
        )

    def first(h):
        for copy in loads(h):
            copy.wait()
        q = q_copies(h)
        kv = kv_copies(h)
        for plan, indices in ((q, (0, 1, 2)), (kv, (0, 1, 2, 3))):
            for index in indices:
                plan[index].start()

    def second(h):
        q = q_copies(h)
        kv = kv_copies(h)
        kv[0].wait_recv()
        kv[4].start()
        kv[1].wait_recv()
        kv[5].start()
        q[1].wait_recv()
        q[5].start()
        q[0].wait_recv()
        q[3].start()
        q[4].start()

    def third(h):
        q = q_copies(h)
        q[3].wait_recv()
        q[6].start()

    def attention(h):
        par = h % 2
        q = q_copies(h)
        kv = kv_copies(h)
        late = (h >= TURN).astype(jnp.int32)

        def arrived(plan, indices):
            for index in indices:
                plan[index].wait_recv()

        def score(index, dest):
            block = (index + 2 * late) % 4
            queries = qbuf[h, pl.ds(pl.multiple_of(block * 2 * ROWS, 2 * ROWS), 2 * ROWS), :]
            dest[...] = dot_nt(kbuf[h], queries)

        def weigh(index, source):
            block = (index + 2 * late) % 4
            scores = source[...].reshape(KB, BLOCK, 2 * ROWS)
            hidden = pen[par, block]
            tops = jnp.max(scores, axis=1) * LOG2 - hidden
            peak = jnp.maximum(jnp.max(tops, axis=0, keepdims=True), FLOOR)
            peak = peak.astype(jnp.bfloat16).astype(jnp.float32)
            shift = peak + hidden
            weights = jnp.exp2(scores * LOG2 - shift[:, None, :]).astype(jnp.bfloat16)
            result = jnp.dot(
                vt[...], weights.reshape(KEYS, 2 * ROWS), preferred_element_type=jnp.float32
            )
            numer = result[0:HD, :].astype(jnp.bfloat16)
            stats = stat_rows(peak, result[HD : HD + 1, :])
            for half in range(2):
                lanes = slice(half * ROWS, (half + 1) * ROWS)
                pbuf[h, block * 2 + half, 0:HD, :] = numer[:, lanes]
                pbuf[h, block * 2 + half, HD:MSG, :] = stats[:, lanes]

        arrived(kv, (2, 3, 4, 5))
        arrived(q, (2, 5))

        @pl.when(late == 1)
        def _():
            arrived(q, (4, 6))

        vt[0:HD, :] = vbuf[h].T
        score(0, sa)
        score(1, sb)
        weigh(0, sa)

        @pl.when(h == 0)
        def _():
            second(2)
            third(1)

        @pl.when(late == 0)
        def _():
            arrived(q, (4, 6))

        score(2, sa)
        weigh(1, sb)
        for place in (2, 3, 1):
            o_copy(h, late, place).start()
        score(3, sb)
        weigh(2, sa)
        weigh(3, sb)
        for place in (2, 3, 1):
            o_copy(h, 1 - late, place).start()

    def put(h, index, parts):
        numer, peak, total = merge(parts)
        pbuf[h, index, 0:HD, :] = numer.astype(jnp.bfloat16)
        pbuf[h, index, HD:MSG, :] = stat_rows(peak, total)

    def take(h, indices):
        return [unpack(ibuf[h, index]) for index in indices]

    def fold(h):
        o = o_copies(h)

        @pl.when(h < DIRECT)
        def _():
            for source, mine, nxt in ((0, 2, 4), (1, 7, 5)):
                o[source].wait_recv()
                put(h, mine, [unpack(pbuf[h, mine])] + take(h, (source,)))
                o[nxt].start()

    def cross(h):
        for side in (1, 0):
            for place in (1, 2, 3):
                o_copy(h, side, place).wait_recv()
            put(h, RING * side, [unpack(pbuf[h, RING * side])] + take(h, range(side * 3, side * 3 + 3)))
            o_flip(h, side).start()

    def finish(h):
        cols = pl.ds(pl.multiple_of(h * HD, HD), HD)
        ready = []
        for side in range(2):
            o_flip(h, 1 - side).wait_recv()
            numer, peak, total = merge([unpack(pbuf[h, RING * side])] + take(h, (6 + side,)))
            ready.append((numer / total).T)
        mine, theirs = ready

        def chosen(delta):
            return jnp.where(z_side(delta) == 1, theirs, mine).astype(jnp.bfloat16)

        att[0, :, cols] = mine.astype(jnp.bfloat16)
        att[1, :, cols] = chosen(1)
        att[2, :, cols] = chosen(-1)
        att[3, 0:HALF, cols] = chosen(2)[0:HALF]
        att[3, HALF:ROWS, cols] = chosen(-2)[HALF:ROWS]

    def prepare():
        vt[HD:MSG, :] = jnp.ones((MSG - HD, KEYS), jnp.bfloat16)
        groups = sees_ref.shape[0]
        table = (
            (lax.broadcasted_iota(jnp.int32, (groups, NBLK), 0) == group_ref[...].reshape(1, NBLK))
            .astype(jnp.float32)
            .astype(jnp.bfloat16)
        )
        allowed = sees_ref[...].astype(jnp.float32).astype(jnp.bfloat16)
        for par in range(2):
            row = lax.broadcasted_iota(jnp.int32, (KB, NBLK), 0)
            slot = row // 4
            if par == 0:
                source = y * 8 + s * 4 + (x + 4 - slot) % 4
            else:
                source = ((y + 4 - slot) % 4) * 8 + s * 4 + x
            key_block = source * 2 + row % 2 + ((row // 2) % 2) * (NBLK // 2)
            picks = (
                (lax.broadcasted_iota(jnp.int32, (KB, NBLK), 1) == key_block)
                .astype(jnp.float32)
                .astype(jnp.bfloat16)
            )
            key_group = dot_nt(picks, table).astype(jnp.bfloat16)
            seen_by = dot_nt(key_group, allowed).astype(jnp.bfloat16)
            for place in range(RING):
                lane = lax.broadcasted_iota(jnp.int32, (NBLK, 2 * ROWS), 1)
                shift = 2 * (place % 2) + lane // ROWS
                side = 1 - s if place >= 2 else s
                if par == 0:
                    origin = ((y + 4 - shift) % 4) * 8 + side * 4 + x
                else:
                    origin = y * 8 + side * 4 + (x + 4 - shift) % 4
                query_block = NBLK // 2 + origin * 2 + (lane // BLOCK) % 2
                wanted = (
                    (lax.broadcasted_iota(jnp.int32, (NBLK, 2 * ROWS), 0) == query_block)
                    .astype(jnp.float32)
                    .astype(jnp.bfloat16)
                )
                query_group = jnp.dot(table, wanted, preferred_element_type=jnp.float32).astype(
                    jnp.bfloat16
                )
                visible = jnp.dot(seen_by, query_group, preferred_element_type=jnp.float32)
                pen[par, place] = jnp.where(visible > 0.5, 0.0, BIG)

    first(0)
    first(1)
    prepare()
    w_copy.start()
    first(2)
    second(0)
    first(3)
    second(1)
    third(0)

    def project(index, side, low, high):
        turn = index + (index // 2) * (5 - 2 * index)
        block = 2 * ((zl + turn) % HEADS_Z) + side
        cols = pl.ds(pl.multiple_of(block * FEAT, FEAT), FEAT)
        rows = slice(low * HD, high * HD)
        return jnp.dot(att[index, :, rows], wbuf[rows, cols], preferred_element_type=jnp.float32)

    def begin(side):
        @pl.loop(0, HEADS_Z)
        def _(index):
            acc[side, index] = project(index, side, 0, EARLY)

    def start_projection(h):
        w_copy.wait()
        begin(1 - core)

    def go_on_projection(h):
        begin(core)

    stages = (
        (third, -1, 2, NH),
        (attention, 0, 0, NH),
        (first, -4, 4, NH),
        (second, -3, 3, NH),
        (start_projection, 1, NH - 1, NH),
        (cross, 1, 0, NH),
        (finish, 2, 0, NH),
        (go_on_projection, 2, NH - 2, NH - 1),
    )

    @pl.loop(0, NH + 2)
    def _(it):
        for stage, lag, low, high in stages:
            @pl.when((it >= lag + low) & (it < high + lag))
            def _():
                stage(it - lag)

    def pair_copy(index):
        return remote(pst.at[index], pin.at[index], p_send.at[index], p_recv.at[index], head=other)

    def line_copy(index):
        device = z_up if index % 2 == 0 else z_down
        return remote(rst.at[index], rin.at[index], r_send.at[index], r_recv.at[index], **device)

    def theirs(index):
        part = acc[1 - core, index] + project(index, 1 - core, EARLY, NH)
        pst[index] = part.astype(jnp.bfloat16)
        pair_copy(index).start()

    def mine(index):
        part = acc[core, index] + project(index, core, EARLY, NH)
        pair_copy(index).wait_recv()
        return part + pin[index].astype(jnp.float32)

    def send(index, value):
        rst[index] = value.astype(jnp.bfloat16)
        line_copy(index).start()

    theirs(3)
    theirs(1)
    far = mine(3)
    send(0, far[0:HALF])
    send(1, far[HALF:ROWS])
    theirs(2)
    above = mine(1)
    send(2, above[HALF:ROWS])
    own[0] = above[0:HALF]
    theirs(0)
    below = mine(2)
    send(3, below[0:HALF])
    own[1] = below[HALF:ROWS]
    for index in range(2):
        line_copy(index).wait_recv()
        send(4 + index, own[index] + rin[index].astype(jnp.float32))
    total = mine(0)
    scale = gate_ref[...].reshape(1, FEAT)
    for index, rows in ((3, slice(0, HALF)), (2, slice(HALF, ROWS))):
        line_copy(index).wait_recv()
        own[3 - index] = total[rows] + rin[index].astype(jnp.float32)
    for index, rows in ((4, slice(0, HALF)), (5, slice(HALF, ROWS))):
        line_copy(index).wait_recv()
        out_ref[rows, :] = ((own[index - 4] + rin[index].astype(jnp.float32)) * scale).astype(jnp.bfloat16)

    @pl.loop(0, NH)
    def _(h):
        for plan in (kv_copies(h), q_copies(h)):
            for index in range(len(plan)):
                plan[index].wait_send()
        for side in range(2):
            for place in (1, 2, 3):
                o_copy(h, side, place).wait_send()
            o_flip(h, side).wait_send()

    for index in range(HEADS_Z):
        pair_copy(index).wait_send()
    for index in range(6):
        line_copy(index).wait_send()


def body(
    queries,
    window_keys,
    window_values,
    context_keys,
    context_values,
    block_group,
    sees,
    out_weight,
    gate,
):
    hbm = pl.BlockSpec(memory_space=pl.ANY)
    vmem = pl.BlockSpec(memory_space=pltpu.VMEM)
    dma = pltpu.SemaphoreType.DMA
    width = out_weight.shape[1]
    bf16 = jnp.bfloat16
    return pl.pallas_call(
        kernel,
        out_shape=jax.ShapeDtypeStruct((ROWS, FEAT), bf16),
        in_specs=[hbm] * 5 + [vmem, vmem, hbm, vmem],
        out_specs=vmem,
        scratch_shapes=[
            pltpu.VMEM((NH, QCH * ROWS, HD), bf16),
            pltpu.VMEM((NH, KEYS, HD), bf16),
            pltpu.VMEM((NH, KEYS, HD), bf16),
            pltpu.VMEM((MSG, KEYS), bf16),
            pltpu.VMEM((2, RING, KB, 2 * ROWS), jnp.float32),
            pltpu.VMEM((NH, QCH, MSG, HD), bf16),
            pltpu.VMEM((NH, 8, MSG, HD), bf16),
            pltpu.VMEM((4, ROWS, FEAT), bf16),
            pltpu.VMEM((FEAT, width), bf16),
            pltpu.VMEM((KEYS, 2 * ROWS), jnp.float32),
            pltpu.VMEM((KEYS, 2 * ROWS), jnp.float32),
            pltpu.VMEM((2, HEADS_Z, ROWS, FEAT), jnp.float32),
            pltpu.VMEM((HEADS_Z, ROWS, FEAT), bf16),
            pltpu.VMEM((HEADS_Z, ROWS, FEAT), bf16),
            pltpu.VMEM((2, HALF, FEAT), jnp.float32),
            pltpu.VMEM((6, HALF, FEAT), bf16),
            pltpu.VMEM((6, HALF, FEAT), bf16),
            dma((NH, 5)),
            dma(()),
            dma((NH, 6)),
            dma((NH, 2, 3)),
            dma((NH, 7)),
            dma((NH, 8)),
            dma((NH, 8)),
            dma((NH, 8)),
            dma((HEADS_Z,)),
            dma((HEADS_Z,)),
            dma((6,)),
            dma((6,)),
        ],
        compiler_params=pltpu.CompilerParams(
            collective_id=0, has_side_effects=True, vmem_limit_bytes=56 * 1024 * 1024
        ),
    )(
        queries,
        window_keys,
        window_values,
        context_keys,
        context_values,
        block_group,
        sees,
        out_weight,
        gate,
    )


def solution(mesh):
    placed = (
        P("tm", "head"),
        P("tm", "head"),
        P("tm", "head"),
        P("tm", "head"),
        P("tm", "head"),
        P(),
        P(),
        P("head", None),
        P("head"),
    )
    return jax.shard_map(
        body, mesh=mesh, in_specs=placed, out_specs=P("tm", "head"), check_vma=False
    )
```

```python
import functools
import math

import jax
import jax.numpy as jnp
from jax import lax
from jax.experimental import pallas as pl
from jax.experimental.pallas import tpu as pltpu
from jax.sharding import PartitionSpec as P

HD = 128
BLOCK = 64
ROWS = 128
NH = 6
FEAT = NH * HD
RING = 4
KEYS = 2 * ROWS * RING
KB = KEYS // BLOCK
QCH = 2 * RING
MSG = HD + 16
HEADS_Z = 4
NBLK = 128
HALF = ROWS // 2
EARLY = 4
TURN = 4
BIG = 1e30
FLOOR = -1e29
MESH = pl.DeviceIdType.MESH
LOG2 = math.log2(math.e) / math.sqrt(HD)


def remote(src, dst, send, recv, **device):
    return pltpu.make_async_remote_copy(
        src_ref=src, dst_ref=dst, send_sem=send, recv_sem=recv, device_id=device, device_id_type=MESH
    )


class Plan:
    def __init__(self, *entries):
        self.entries = entries

    def __getitem__(self, index):
        src, dst, send, recv, peer = self.entries[index]
        return remote(src, dst, send, recv, tm=peer)

    def __len__(self):
        return len(self.entries)


def dot_nt(a, b):
    return lax.dot_general(a, b, (((1,), (1,)), ((), ())), preferred_element_type=jnp.float32)


def unpack(message):
    stats = message[HD:MSG, :].astype(jnp.float32)
    return (message[0:HD, :].astype(jnp.float32), stats[0:1, :], stats[1:2, :] + stats[2:3, :])


def merge(parts):
    peak = parts[0][1]
    for part in parts[1:]:
        peak = jnp.maximum(peak, part[1])
    numer = None
    total = None
    for part in parts:
        factor = jnp.exp2(part[1] - peak)
        numer = part[0] * factor if numer is None else numer + part[0] * factor
        total = part[2] * factor if total is None else total + part[2] * factor
    return (numer, peak, total)


def stat_rows(peak, total):
    high = total.astype(jnp.bfloat16).astype(jnp.float32)
    rows = lax.broadcasted_iota(jnp.int32, (MSG - HD, peak.shape[1]), 0)
    picked = jnp.where(rows == 0, peak, jnp.where(rows == 1, high, total - high))
    return picked.astype(jnp.bfloat16)


def kernel(
    q_hbm,
    wk_hbm,
    wv_hbm,
    ck_hbm,
    cv_hbm,
    group_ref,
    sees_ref,
    w_hbm,
    gate_ref,
    out_ref,
    qbuf,
    kbuf,
    vbuf,
    vt,
    pen,
    pbuf,
    ibuf,
    att,
    wbuf,
    sa,
    sb,
    acc,
    pst,
    pin,
    own,
    rst,
    rin,
    load_sem,
    w_sem,
    kv_send,
    kv_recv,
    q_send,
    q_recv,
    o_send,
    o_recv,
    p_send,
    p_recv,
    r_send,
    r_recv,
):
    t = lax.axis_index("tm")
    hd = lax.axis_index("head")
    x = t % 4
    s = (t // 4) % 2
    y = t // 8
    zl = hd // 2
    core = hd % 2
    flip = t + 4 - 8 * s
    other = hd + 1 - 2 * core
    z = s * HEADS_Z + zl

    def z_device(delta):
        place = (z + delta + 8) % 8
        return {"tm": t + (place // HEADS_Z - s) * 4, "head": (place % HEADS_Z) * 2 + core}

    def z_side(delta):
        return (((z + delta + 8) % 8) // HEADS_Z + s) % 2

    z_up = z_device(1)
    z_down = z_device(-1)

    def along(delta):
        return (t - x + (x + delta + 4) % 4, t + ((y + delta + 4) % 4 - y) * 8)

    x_up, y_up = along(1)
    x_down, y_down = along(-1)

    def kv_peer(par, up):
        a, b = (x_up, y_up) if up else (x_down, y_down)
        return a * (1 - par) + b * par

    def far_peer(par):
        a, b = along(2)
        return a * par + b * (1 - par)

    def q_peer(par, up):
        a, b = (x_up, y_up) if up else (x_down, y_down)
        return a * par + b * (1 - par)

    def loads(h):
        cols = pl.ds(pl.multiple_of(h * HD, HD), HD)
        return (
            pltpu.make_async_copy(q_hbm.at[:, cols], qbuf.at[h, 0:ROWS], load_sem.at[h]),
            pltpu.make_async_copy(ck_hbm.at[:, cols], kbuf.at[h, 0:ROWS], load_sem.at[h]),
            pltpu.make_async_copy(wk_hbm.at[:, cols], kbuf.at[h, ROWS : 2 * ROWS], load_sem.at[h]),
            pltpu.make_async_copy(cv_hbm.at[:, cols], vbuf.at[h, 0:ROWS], load_sem.at[h]),
            pltpu.make_async_copy(wv_hbm.at[:, cols], vbuf.at[h, ROWS : 2 * ROWS], load_sem.at[h]),
        )

    @pl.loop(0, NH)
    def _(h):
        for copy in loads(h):
            copy.start()

    w_copy = pltpu.make_async_copy(w_hbm, wbuf, w_sem)

    barrier = pltpu.get_barrier_semaphore()
    x_far, y_far = along(2)
    for peer in (x_up, x_down, y_up, y_down, flip, x_far, y_far):
        pl.semaphore_signal(barrier, inc=1, device_id={"tm": peer}, device_id_type=MESH)
    pl.semaphore_signal(barrier, inc=1, device_id={"head": other}, device_id_type=MESH)
    for device in (z_up, z_down):
        pl.semaphore_signal(barrier, inc=1, device_id=device, device_id_type=MESH)
    pl.semaphore_wait(barrier, 10)

    def kslot(buf, h, slot):
        return buf.at[h, slot * 2 * ROWS : (slot + 1) * 2 * ROWS]

    def chunk(h, index):
        return qbuf.at[h, index * ROWS : (index + 1) * ROWS]

    def kv_copies(h):
        up = kv_peer(h % 2, True)
        down = kv_peer(h % 2, False)
        def one(buf, src, dst, kind, arrival, peer):
            return (kslot(buf, h, src), kslot(buf, h, dst), kv_send.at[kind], kv_recv.at[h, arrival], peer)

        return Plan(
            one(kbuf, 0, 1, 0, 0, up),
            one(vbuf, 0, 3, 1, 1, down),
            one(vbuf, 0, 1, 1, 2, up),
            one(kbuf, 0, 3, 0, 2, down),
            one(kbuf, 1, 2, 0, 2, up),
            one(vbuf, 3, 2, 1, 2, down),
        )

    def q_copies(h):
        up = q_peer(h % 2, True)
        down = q_peer(h % 2, False)

        def one(src, dst, arrival, peer):
            return (chunk(h, src), chunk(h, dst), q_send, q_recv.at[h, arrival], peer)

        return Plan(
            one(0, 4, 0, flip),
            one(0, 1, 1, up),
            one(0, 3, 3, down),
            one(4, 7, 2, down),
            one(4, 5, 4, up),
            one(1, 2, 3, up),
            one(7, 6, 4, down),
        )

    def o_copy(h, side, place):
        peer = (q_peer(h % 2, False), far_peer(h % 2), q_peer(h % 2, True))[place - 1]
        slot = side * 3 + place - 1
        return remote(
            pbuf.at[h, side * RING + place], ibuf.at[h, slot], o_send, o_recv.at[h, side], tm=peer
        )

    def o_flip(h, side):
        return remote(
            pbuf.at[h, RING * side],
            ibuf.at[h, 7 - side],
            o_send,
            o_recv.at[h, 3 - side],
            tm=flip,
        )

    def first(h):
        pltpu.make_async_copy(qbuf.at[h, 0 : 5 * ROWS], qbuf.at[h, 0 : 5 * ROWS], load_sem.at[h]).wait()
        q = q_copies(h)
        kv = kv_copies(h)
        for plan, indices in ((q, (0, 1, 2)), (kv, (0, 1, 2, 3))):
            for index in indices:
                plan[index].start()

    def second(h):
        q = q_copies(h)
        kv = kv_copies(h)
        kv[0].wait_recv()
        kv[4].start()
        kv[1].wait_recv()
        kv[5].start()
        q[1].wait_recv()
        q[5].start()
        q[0].wait_recv()
        q[3].start()
        q[4].start()

    def third(h):
        q = q_copies(h)
        q[3].wait_recv()
        q[6].start()

    def attention(h):
        par = h % 2
        late = (h >= TURN).astype(jnp.int32)

        def arrived(ref, sem):
            pltpu.make_async_copy(ref, ref, sem).wait()

        def pair(h, arrival):
            ref = qbuf.at[h, 0 : 2 * ROWS]
            arrived(ref, q_recv.at[h, arrival])

        def score(index, dest):
            block = (index + 2 * late) % 4
            queries = qbuf[h, pl.ds(pl.multiple_of(block * 2 * ROWS, 2 * ROWS), 2 * ROWS), :]
            dest[...] = dot_nt(kbuf[h], queries)

        def weigh(index, source):
            block = (index + 2 * late) % 4
            scores = source[...].reshape(KB, BLOCK, 2 * ROWS)
            hidden = pen[par, block]
            tops = jnp.max(scores, axis=1) * LOG2 - hidden
            peak = jnp.maximum(jnp.max(tops, axis=0, keepdims=True), FLOOR)
            peak = peak.astype(jnp.bfloat16).astype(jnp.float32)
            shift = peak + hidden
            weights = jnp.exp2(scores * LOG2 - shift[:, None, :]).astype(jnp.bfloat16)
            result = jnp.dot(
                vt[...], weights.reshape(KEYS, 2 * ROWS), preferred_element_type=jnp.float32
            )
            numer = result[0:HD, :].astype(jnp.bfloat16)
            stats = stat_rows(peak, result[HD : HD + 1, :])
            for half in range(2):
                lanes = slice(half * ROWS, (half + 1) * ROWS)
                pbuf[h, block * 2 + half, 0:HD, :] = numer[:, lanes]
                pbuf[h, block * 2 + half, HD:MSG, :] = stats[:, lanes]

        arrived(kbuf.at[h], kv_recv.at[h, 2])
        pair(h, 3)

        @pl.when(late == 1)
        def _():
            pair(h, 4)

        vt[0:HD, :] = vbuf[h].T
        score(0, sa)
        score(1, sb)
        weigh(0, sa)

        @pl.when(h == 0)
        def _():
            second(2)
            third(1)

        @pl.when(late == 0)
        def _():
            pair(h, 4)

        score(2, sa)
        weigh(1, sb)
        for place in (2, 3, 1):
            o_copy(h, late, place).start()
        score(3, sb)
        weigh(2, sa)
        weigh(3, sb)
        for place in (2, 3, 1):
            o_copy(h, 1 - late, place).start()

    def put(h, index, parts):
        numer, peak, total = merge(parts)
        pbuf[h, index, 0:HD, :] = numer.astype(jnp.bfloat16)
        pbuf[h, index, HD:MSG, :] = stat_rows(peak, total)

    def take(h, indices):
        return [unpack(ibuf[h, index]) for index in indices]

    def fold(h):
        o = o_copies(h)

        @pl.when(h < DIRECT)
        def _():
            for source, mine, nxt in ((0, 2, 4), (1, 7, 5)):
                o[source].wait_recv()
                put(h, mine, [unpack(pbuf[h, mine])] + take(h, (source,)))
                o[nxt].start()

    def cross(h):
        for side in (1, 0):
            landed = ibuf.at[h, side * 3 : side * 3 + 3]
            pltpu.make_async_copy(landed, landed, o_recv.at[h, side]).wait()
            put(h, RING * side, [unpack(pbuf[h, RING * side])] + take(h, range(side * 3, side * 3 + 3)))
            o_flip(h, side).start()

    def finish(h):
        cols = pl.ds(pl.multiple_of(h * HD, HD), HD)
        ready = []
        for side in range(2):
            o_flip(h, 1 - side).wait_recv()
            numer, peak, total = merge([unpack(pbuf[h, RING * side])] + take(h, (6 + side,)))
            ready.append((numer / total).T)
        mine, theirs = ready

        def chosen(delta):
            return jnp.where(z_side(delta) == 1, theirs, mine).astype(jnp.bfloat16)

        att[0, :, cols] = mine.astype(jnp.bfloat16)
        att[1, :, cols] = chosen(1)
        att[2, :, cols] = chosen(-1)
        att[3, 0:HALF, cols] = chosen(2)[0:HALF]
        att[3, HALF:ROWS, cols] = chosen(-2)[HALF:ROWS]

    def prepare():
        vt[HD:MSG, :] = jnp.ones((MSG - HD, KEYS), jnp.bfloat16)
        groups = sees_ref.shape[0]
        table = (
            (lax.broadcasted_iota(jnp.int32, (groups, NBLK), 0) == group_ref[...].reshape(1, NBLK))
            .astype(jnp.float32)
            .astype(jnp.bfloat16)
        )
        allowed = sees_ref[...].astype(jnp.float32).astype(jnp.bfloat16)
        for par in range(2):
            row = lax.broadcasted_iota(jnp.int32, (KB, NBLK), 0)
            slot = row // 4
            if par == 0:
                source = y * 8 + s * 4 + (x + 4 - slot) % 4
            else:
                source = ((y + 4 - slot) % 4) * 8 + s * 4 + x
            key_block = source * 2 + row % 2 + ((row // 2) % 2) * (NBLK // 2)
            picks = (
                (lax.broadcasted_iota(jnp.int32, (KB, NBLK), 1) == key_block)
                .astype(jnp.float32)
                .astype(jnp.bfloat16)
            )
            key_group = dot_nt(picks, table).astype(jnp.bfloat16)
            seen_by = dot_nt(key_group, allowed).astype(jnp.bfloat16)
            for place in range(RING):
                lane = lax.broadcasted_iota(jnp.int32, (NBLK, 2 * ROWS), 1)
                shift = 2 * (place % 2) + lane // ROWS
                side = 1 - s if place >= 2 else s
                if par == 0:
                    origin = ((y + 4 - shift) % 4) * 8 + side * 4 + x
                else:
                    origin = y * 8 + side * 4 + (x + 4 - shift) % 4
                query_block = NBLK // 2 + origin * 2 + (lane // BLOCK) % 2
                wanted = (
                    (lax.broadcasted_iota(jnp.int32, (NBLK, 2 * ROWS), 0) == query_block)
                    .astype(jnp.float32)
                    .astype(jnp.bfloat16)
                )
                query_group = jnp.dot(table, wanted, preferred_element_type=jnp.float32).astype(
                    jnp.bfloat16
                )
                visible = jnp.dot(seen_by, query_group, preferred_element_type=jnp.float32)
                pen[par, place] = jnp.where(visible > 0.5, 0.0, BIG)

    first(0)
    first(1)
    prepare()
    w_copy.start()
    first(2)
    second(0)
    first(3)
    second(1)
    first(4)
    third(0)
    first(5)

    def project(index, side, low, high):
        turn = index + (index // 2) * (5 - 2 * index)
        block = 2 * ((zl + turn) % HEADS_Z) + side
        cols = pl.ds(pl.multiple_of(block * FEAT, FEAT), FEAT)
        rows = slice(low * HD, high * HD)
        return jnp.dot(att[index, :, rows], wbuf[rows, cols], preferred_element_type=jnp.float32)

    def begin(side):
        @pl.loop(0, HEADS_Z)
        def _(index):
            acc[side, index] = project(index, side, 0, EARLY)

    def start_projection(h):
        w_copy.wait()
        begin(1 - core)

    def go_on_projection(h):
        begin(core)

    stages = (
        (third, -1, 2, NH),
        (attention, 0, 0, NH),
        (second, -3, 3, NH),
        (finish, 3, 0, NH),
        (start_projection, 1, NH - 1, NH),
        (cross, 1, 0, NH),
        (go_on_projection, 1, NH - 1, NH),
    )

    @pl.loop(0, NH + 3)
    def _(it):
        for stage, lag, low, high in stages:
            @pl.when((it >= lag + low) & (it < high + lag))
            def _():
                stage(it - lag)

    def pair_copy(index):
        return remote(pst.at[index], pin.at[index], p_send.at[index], p_recv.at[index], head=other)

    def line_copy(index):
        device = z_up if index % 2 == 0 else z_down
        return remote(rst.at[index], rin.at[index], r_send.at[index], r_recv.at[index], **device)

    def theirs(index):
        part = acc[1 - core, index] + project(index, 1 - core, EARLY, NH)
        pst[index] = part.astype(jnp.bfloat16)
        pair_copy(index).start()

    def mine(index):
        part = acc[core, index] + project(index, core, EARLY, NH)
        pair_copy(index).wait_recv()
        return part + pin[index].astype(jnp.float32)

    def send(index, value):
        rst[index] = value.astype(jnp.bfloat16)
        line_copy(index).start()

    theirs(3)
    theirs(1)
    far = mine(3)
    send(0, far[0:HALF])
    send(1, far[HALF:ROWS])
    theirs(2)
    above = mine(1)
    send(2, above[HALF:ROWS])
    own[0] = above[0:HALF]
    theirs(0)
    below = mine(2)
    send(3, below[0:HALF])
    own[1] = below[HALF:ROWS]
    for index in range(2):
        line_copy(index).wait_recv()
        send(4 + index, own[index] + rin[index].astype(jnp.float32))
    total = mine(0)
    scale = gate_ref[...].reshape(1, FEAT)
    for index, rows in ((3, slice(0, HALF)), (2, slice(HALF, ROWS))):
        line_copy(index).wait_recv()
        own[3 - index] = total[rows] + rin[index].astype(jnp.float32)
    for index, rows in ((4, slice(0, HALF)), (5, slice(HALF, ROWS))):
        line_copy(index).wait_recv()
        out_ref[rows, :] = ((own[index - 4] + rin[index].astype(jnp.float32)) * scale).astype(jnp.bfloat16)

    for ref, sem in (
        (kbuf.at[:, 0 : 6 * ROWS], kv_send.at[0]),
        (vbuf.at[:, 0 : 6 * ROWS], kv_send.at[1]),
        (qbuf.at[:, 0 : 7 * ROWS], q_send),
        (pbuf, o_send),
    ):
        pltpu.make_async_copy(ref, ref, sem).wait()

    for index in range(HEADS_Z):
        pair_copy(index).wait_send()
    for index in range(6):
        line_copy(index).wait_send()


def body(
    queries,
    window_keys,
    window_values,
    context_keys,
    context_values,
    block_group,
    sees,
    out_weight,
    gate,
):
    hbm = pl.BlockSpec(memory_space=pl.ANY)
    vmem = pl.BlockSpec(memory_space=pltpu.VMEM)
    dma = pltpu.SemaphoreType.DMA
    width = out_weight.shape[1]
    bf16 = jnp.bfloat16
    return pl.pallas_call(
        kernel,
        out_shape=jax.ShapeDtypeStruct((ROWS, FEAT), bf16),
        in_specs=[hbm] * 5 + [vmem, vmem, hbm, vmem],
        out_specs=vmem,
        scratch_shapes=[
            pltpu.VMEM((NH, QCH * ROWS, HD), bf16),
            pltpu.VMEM((NH, KEYS, HD), bf16),
            pltpu.VMEM((NH, KEYS, HD), bf16),
            pltpu.VMEM((MSG, KEYS), bf16),
            pltpu.VMEM((2, RING, KB, 2 * ROWS), jnp.float32),
            pltpu.VMEM((NH, QCH, MSG, HD), bf16),
            pltpu.VMEM((NH, 8, MSG, HD), bf16),
            pltpu.VMEM((4, ROWS, FEAT), bf16),
            pltpu.VMEM((FEAT, width), bf16),
            pltpu.VMEM((KEYS, 2 * ROWS), jnp.float32),
            pltpu.VMEM((KEYS, 2 * ROWS), jnp.float32),
            pltpu.VMEM((2, HEADS_Z, ROWS, FEAT), jnp.float32),
            pltpu.VMEM((HEADS_Z, ROWS, FEAT), bf16),
            pltpu.VMEM((HEADS_Z, ROWS, FEAT), bf16),
            pltpu.VMEM((2, HALF, FEAT), jnp.float32),
            pltpu.VMEM((6, HALF, FEAT), bf16),
            pltpu.VMEM((6, HALF, FEAT), bf16),
            dma((NH,)),
            dma(()),
            dma((2,)),
            dma((NH, 3)),
            dma(()),
            dma((NH, 5)),
            dma(()),
            dma((NH, 4)),
            dma((HEADS_Z,)),
            dma((HEADS_Z,)),
            dma((6,)),
            dma((6,)),
        ],
        compiler_params=pltpu.CompilerParams(
            collective_id=0, has_side_effects=True, vmem_limit_bytes=56 * 1024 * 1024
        ),
    )(
        queries,
        window_keys,
        window_values,
        context_keys,
        context_values,
        block_group,
        sees,
        out_weight,
        gate,
    )


def solution(mesh):
    placed = (
        P("tm", "head"),
        P("tm", "head"),
        P("tm", "head"),
        P("tm", "head"),
        P("tm", "head"),
        P(),
        P(),
        P("head", None),
        P("head"),
    )
    return jax.shard_map(
        body, mesh=mesh, in_specs=placed, out_specs=P("tm", "head"), check_vma=False
    )
```

```python
import functools
import math

import jax
import jax.numpy as jnp
from jax import lax
from jax.experimental import pallas as pl
from jax.experimental.pallas import tpu as pltpu
from jax.sharding import PartitionSpec as P

HD = 128
BLOCK = 64
ROWS = 128
NH = 6
FEAT = NH * HD
RING = 4
KEYS = 2 * ROWS * RING
KB = KEYS // BLOCK
QCH = 2 * RING
MSG = HD + 16
HEADS_Z = 4
NBLK = 128
HALF = ROWS // 2
EARLY = 2
LATER = 4
TURN = 4
STRAIGHT = 3
BIG = 1e30
FLOOR = -1e29
MESH = pl.DeviceIdType.MESH
LOG2 = math.log2(math.e) / math.sqrt(HD)


def remote(src, dst, send, recv, **device):
    return pltpu.make_async_remote_copy(
        src_ref=src, dst_ref=dst, send_sem=send, recv_sem=recv, device_id=device, device_id_type=MESH
    )


class Plan:
    def __init__(self, *entries):
        self.entries = entries

    def __getitem__(self, index):
        src, dst, send, recv, peer = self.entries[index]
        return remote(src, dst, send, recv, tm=peer)

    def __len__(self):
        return len(self.entries)


def dot_nt(a, b):
    return lax.dot_general(a, b, (((1,), (1,)), ((), ())), preferred_element_type=jnp.float32)


def unpack(message):
    stats = message[HD:MSG, :].astype(jnp.float32)
    return (message[0:HD, :].astype(jnp.float32), stats[0:1, :], stats[1:2, :] + stats[2:3, :])


def merge(parts):
    peak = parts[0][1]
    for part in parts[1:]:
        peak = jnp.maximum(peak, part[1])
    numer = None
    total = None
    for part in parts:
        factor = jnp.exp2(part[1] - peak)
        numer = part[0] * factor if numer is None else numer + part[0] * factor
        total = part[2] * factor if total is None else total + part[2] * factor
    return (numer, peak, total)


def stat_rows(peak, total):
    high = total.astype(jnp.bfloat16).astype(jnp.float32)
    rows = lax.broadcasted_iota(jnp.int32, (MSG - HD, peak.shape[1]), 0)
    picked = jnp.where(rows == 0, peak, jnp.where(rows == 1, high, total - high))
    return picked.astype(jnp.bfloat16)


def kernel(
    q_hbm,
    wk_hbm,
    wv_hbm,
    ck_hbm,
    cv_hbm,
    group_ref,
    sees_ref,
    w_hbm,
    gate_ref,
    out_ref,
    qbuf,
    kbuf,
    vbuf,
    vt,
    pen,
    pbuf,
    ibuf,
    att,
    wbuf,
    sa,
    sb,
    acc,
    pst,
    pin,
    own,
    rst,
    rin,
    load_sem,
    w_sem,
    kv_send,
    kv_recv,
    q_send,
    q_recv,
    o_send,
    o_recv,
    p_send,
    p_recv,
    r_send,
    r_recv,
):
    t = lax.axis_index("tm")
    hd = lax.axis_index("head")
    x = t % 4
    s = (t // 4) % 2
    y = t // 8
    zl = hd // 2
    core = hd % 2
    flip = t + 4 - 8 * s
    other = hd + 1 - 2 * core
    z = s * HEADS_Z + zl

    def z_device(delta):
        place = (z + delta + 8) % 8
        return {"tm": t + (place // HEADS_Z - s) * 4, "head": (place % HEADS_Z) * 2 + core}

    def z_side(delta):
        return (((z + delta + 8) % 8) // HEADS_Z + s) % 2

    z_up = z_device(1)
    z_down = z_device(-1)

    def along(delta):
        return (t - x + (x + delta + 4) % 4, t + ((y + delta + 4) % 4 - y) * 8)

    x_up, y_up = along(1)
    x_down, y_down = along(-1)

    def kv_peer(par, up):
        a, b = (x_up, y_up) if up else (x_down, y_down)
        return a * (1 - par) + b * par

    def far_peer(par):
        a, b = along(2)
        return a * par + b * (1 - par)

    def q_peer(par, up):
        a, b = (x_up, y_up) if up else (x_down, y_down)
        return a * par + b * (1 - par)

    def loads(h):
        cols = pl.ds(pl.multiple_of(h * HD, HD), HD)
        return (
            pltpu.make_async_copy(q_hbm.at[:, cols], qbuf.at[h, 0:ROWS], load_sem.at[h]),
            pltpu.make_async_copy(ck_hbm.at[:, cols], kbuf.at[h, 0:ROWS], load_sem.at[h]),
            pltpu.make_async_copy(wk_hbm.at[:, cols], kbuf.at[h, ROWS : 2 * ROWS], load_sem.at[h]),
            pltpu.make_async_copy(cv_hbm.at[:, cols], vbuf.at[h, 0:ROWS], load_sem.at[h]),
            pltpu.make_async_copy(wv_hbm.at[:, cols], vbuf.at[h, ROWS : 2 * ROWS], load_sem.at[h]),
        )

    @pl.loop(0, NH)
    def _(h):
        for copy in loads(h):
            copy.start()

    w_copy = pltpu.make_async_copy(w_hbm, wbuf, w_sem)

    barrier = pltpu.get_barrier_semaphore()
    x_far, y_far = along(2)
    for peer in (x_up, x_down, y_up, y_down, flip, x_far, y_far):
        pl.semaphore_signal(barrier, inc=1, device_id={"tm": peer}, device_id_type=MESH)
    pl.semaphore_signal(barrier, inc=1, device_id={"head": other}, device_id_type=MESH)
    for device in (z_up, z_down):
        pl.semaphore_signal(barrier, inc=1, device_id=device, device_id_type=MESH)
    pl.semaphore_wait(barrier, 10)

    def kslot(buf, h, slot):
        return buf.at[h, slot * 2 * ROWS : (slot + 1) * 2 * ROWS]

    def chunk(h, index):
        return qbuf.at[h, index * ROWS : (index + 1) * ROWS]

    def kv_copies(h):
        up = kv_peer(h % 2, True)
        down = kv_peer(h % 2, False)
        def one(buf, src, dst, kind, arrival, peer):
            return (kslot(buf, h, src), kslot(buf, h, dst), kv_send.at[kind], kv_recv.at[h, arrival], peer)

        return Plan(
            one(kbuf, 0, 1, 0, 0, up),
            one(vbuf, 0, 3, 1, 1, down),
            one(vbuf, 0, 1, 1, 2, up),
            one(kbuf, 0, 3, 0, 2, down),
            one(kbuf, 1, 2, 0, 2, up),
            one(vbuf, 3, 2, 1, 2, down),
        )

    def q_copies(h):
        up = q_peer(h % 2, True)
        down = q_peer(h % 2, False)

        def one(src, dst, arrival, peer):
            return (chunk(h, src), chunk(h, dst), q_send, q_recv.at[h, arrival], peer)

        return Plan(
            one(0, 4, 0, flip),
            one(0, 1, 1, up),
            one(0, 3, 3, down),
            one(4, 7, 2, down),
            one(4, 5, 4, up),
            one(1, 2, 3, up),
            one(7, 6, 4, down),
            one(4, 6, 4, far_peer(h % 2)),
        )

    def o_copy(h, side, place):
        peer = (q_peer(h % 2, False), far_peer(h % 2), q_peer(h % 2, True))[place - 1]
        slot = side * 3 + place - 1
        return remote(
            pbuf.at[h, side * RING + place], ibuf.at[h, slot], o_send, o_recv.at[h, side], tm=peer
        )

    def o_flip(h, side):
        return remote(
            pbuf.at[h, RING * side],
            ibuf.at[h, 7 - side],
            o_send,
            o_recv.at[h, 3 - side],
            tm=flip,
        )

    def first(h):
        pltpu.make_async_copy(qbuf.at[h, 0 : 5 * ROWS], qbuf.at[h, 0 : 5 * ROWS], load_sem.at[h]).wait()
        q = q_copies(h)
        kv = kv_copies(h)
        for plan, indices in ((q, (0, 1, 2)), (kv, (0, 1, 2, 3))):
            for index in indices:
                plan[index].start()

    def second(h):
        q = q_copies(h)
        kv = kv_copies(h)
        kv[0].wait_recv()
        kv[4].start()
        kv[1].wait_recv()
        kv[5].start()
        q[1].wait_recv()
        q[5].start()
        q[0].wait_recv()
        q[3].start()
        q[4].start()

        @pl.when(h < STRAIGHT)
        def _():
            q[7].start()

    def third(h):
        q = q_copies(h)
        q[3].wait_recv()
        q[6].start()

    def attention(h):
        par = h % 2
        late = (h >= TURN).astype(jnp.int32)

        def arrived(ref, sem):
            pltpu.make_async_copy(ref, ref, sem).wait()

        def pair(h, arrival):
            ref = qbuf.at[h, 0 : 2 * ROWS]
            arrived(ref, q_recv.at[h, arrival])

        def score(index, dest):
            block = (index + 2 * late) % 4
            queries = qbuf[h, pl.ds(pl.multiple_of(block * 2 * ROWS, 2 * ROWS), 2 * ROWS), :]
            dest[...] = dot_nt(kbuf[h], queries)

        def weigh(index, source):
            block = (index + 2 * late) % 4
            scores = source[...].reshape(KB, BLOCK, 2 * ROWS)
            hidden = pen[par, block]
            tops = jnp.max(scores, axis=1) * LOG2 - hidden
            peak = jnp.maximum(jnp.max(tops, axis=0, keepdims=True), FLOOR)
            peak = peak.astype(jnp.bfloat16).astype(jnp.float32)
            shift = peak + hidden
            weights = jnp.exp2(scores * LOG2 - shift[:, None, :]).astype(jnp.bfloat16)
            result = jnp.dot(
                vt[...], weights.reshape(KEYS, 2 * ROWS), preferred_element_type=jnp.float32
            )
            numer = result[0:HD, :].astype(jnp.bfloat16)
            stats = stat_rows(peak, result[HD : HD + 1, :])
            for half in range(2):
                lanes = slice(half * ROWS, (half + 1) * ROWS)
                pbuf[h, block * 2 + half, 0:HD, :] = numer[:, lanes]
                pbuf[h, block * 2 + half, HD:MSG, :] = stats[:, lanes]

        arrived(kbuf.at[h], kv_recv.at[h, 2])
        pair(h, 3)

        @pl.when(late == 1)
        def _():
            pair(h, 4)

        vt[0:HD, :] = vbuf[h].T
        score(0, sa)
        score(1, sb)
        weigh(0, sa)

        @pl.when(h == 0)
        def _():
            second(2)

        @pl.when(late == 0)
        def _():
            pair(h, 4)

        @pl.when(h < STRAIGHT)
        def _():
            arrived(chunk(h, 7), q_recv.at[h, 2])

        score(2, sa)
        weigh(1, sb)
        for place in (2, 3, 1):
            o_copy(h, late, place).start()
        score(3, sb)
        weigh(2, sa)
        weigh(3, sb)
        for place in (2, 3, 1):
            o_copy(h, 1 - late, place).start()

    def put(h, index, parts):
        numer, peak, total = merge(parts)
        pbuf[h, index, 0:HD, :] = numer.astype(jnp.bfloat16)
        pbuf[h, index, HD:MSG, :] = stat_rows(peak, total)

    def take(h, indices):
        return [unpack(ibuf[h, index]) for index in indices]

    def fold(h):
        o = o_copies(h)

        @pl.when(h < DIRECT)
        def _():
            for source, mine, nxt in ((0, 2, 4), (1, 7, 5)):
                o[source].wait_recv()
                put(h, mine, [unpack(pbuf[h, mine])] + take(h, (source,)))
                o[nxt].start()

    def cross(h):
        for side in (1, 0):
            landed = ibuf.at[h, side * 3 : side * 3 + 3]
            pltpu.make_async_copy(landed, landed, o_recv.at[h, side]).wait()
            put(h, RING * side, [unpack(pbuf[h, RING * side])] + take(h, range(side * 3, side * 3 + 3)))
            o_flip(h, side).start()

    def finish(h):
        cols = pl.ds(pl.multiple_of(h * HD, HD), HD)
        ready = []
        for side in range(2):
            o_flip(h, 1 - side).wait_recv()
            numer, peak, total = merge([unpack(pbuf[h, RING * side])] + take(h, (6 + side,)))
            ready.append((numer / total).T)
        mine, theirs = ready

        def chosen(delta):
            return jnp.where(z_side(delta) == 1, theirs, mine).astype(jnp.bfloat16)

        att[0, :, cols] = mine.astype(jnp.bfloat16)
        att[1, :, cols] = chosen(1)
        att[2, :, cols] = chosen(-1)
        att[3, 0:HALF, cols] = chosen(2)[0:HALF]
        att[3, HALF:ROWS, cols] = chosen(-2)[HALF:ROWS]

    def prepare():
        vt[HD:MSG, :] = jnp.ones((MSG - HD, KEYS), jnp.bfloat16)
        groups = sees_ref.shape[0]
        table = (
            (lax.broadcasted_iota(jnp.int32, (groups, NBLK), 0) == group_ref[...].reshape(1, NBLK))
            .astype(jnp.float32)
            .astype(jnp.bfloat16)
        )
        allowed = sees_ref[...].astype(jnp.float32).astype(jnp.bfloat16)
        for par in range(2):
            row = lax.broadcasted_iota(jnp.int32, (KB, NBLK), 0)
            slot = row // 4
            if par == 0:
                source = y * 8 + s * 4 + (x + 4 - slot) % 4
            else:
                source = ((y + 4 - slot) % 4) * 8 + s * 4 + x
            key_block = source * 2 + row % 2 + ((row // 2) % 2) * (NBLK // 2)
            picks = (
                (lax.broadcasted_iota(jnp.int32, (KB, NBLK), 1) == key_block)
                .astype(jnp.float32)
                .astype(jnp.bfloat16)
            )
            key_group = dot_nt(picks, table).astype(jnp.bfloat16)
            seen_by = dot_nt(key_group, allowed).astype(jnp.bfloat16)
            for place in range(RING):
                lane = lax.broadcasted_iota(jnp.int32, (NBLK, 2 * ROWS), 1)
                shift = 2 * (place % 2) + lane // ROWS
                side = 1 - s if place >= 2 else s
                if par == 0:
                    origin = ((y + 4 - shift) % 4) * 8 + side * 4 + x
                else:
                    origin = y * 8 + side * 4 + (x + 4 - shift) % 4
                query_block = NBLK // 2 + origin * 2 + (lane // BLOCK) % 2
                wanted = (
                    (lax.broadcasted_iota(jnp.int32, (NBLK, 2 * ROWS), 0) == query_block)
                    .astype(jnp.float32)
                    .astype(jnp.bfloat16)
                )
                query_group = jnp.dot(table, wanted, preferred_element_type=jnp.float32).astype(
                    jnp.bfloat16
                )
                visible = jnp.dot(seen_by, query_group, preferred_element_type=jnp.float32)
                pen[par, place] = jnp.where(visible > 0.5, 0.0, BIG)

    first(0)
    first(1)
    prepare()
    w_copy.start()
    first(2)
    second(0)
    first(3)
    second(1)
    first(4)
    first(5)

    def project(index, side, low, high):
        turn = index + (index // 2) * (5 - 2 * index)
        block = 2 * ((zl + turn) % HEADS_Z) + side
        cols = pl.ds(pl.multiple_of(block * FEAT, FEAT), FEAT)
        rows = slice(low * HD, high * HD)
        return jnp.dot(att[index, :, rows], wbuf[rows, cols], preferred_element_type=jnp.float32)

    def begin(side):
        @pl.loop(0, HEADS_Z)
        def _(index):
            acc[side, index] = project(index, side, 0, EARLY)

    def extend(side):
        @pl.loop(0, HEADS_Z)
        def _(index):
            acc[side, index] += project(index, side, EARLY, LATER)

    def start_projection(h):
        w_copy.wait()
        begin(0)
        begin(1)

    def go_on_projection(h):
        extend(0)
        extend(1)

    stages = (
        (third, -1, STRAIGHT, NH),
        (attention, 0, 0, NH),
        (second, -3, 3, NH),
        (start_projection, 1, NH - 1, NH),
        (cross, 1, 0, NH),
        (finish, 3, 0, NH),
        (go_on_projection, 1, NH - 1, NH),
    )

    @pl.loop(0, NH + 3)
    def _(it):
        for stage, lag, low, high in stages:
            @pl.when((it >= lag + low) & (it < high + lag))
            def _():
                stage(it - lag)

    def pair_copy(index):
        return remote(pst.at[index], pin.at[index], p_send.at[index], p_recv.at[index], head=other)

    def line_copy(index):
        device = z_up if index % 2 == 0 else z_down
        return remote(rst.at[index], rin.at[index], r_send.at[index], r_recv.at[index], **device)

    def theirs(index):
        part = acc[1 - core, index] + project(index, 1 - core, LATER, NH)
        pst[index] = part.astype(jnp.bfloat16)
        pair_copy(index).start()

    def mine(index):
        part = acc[core, index] + project(index, core, LATER, NH)
        pair_copy(index).wait_recv()
        return part + pin[index].astype(jnp.float32)

    def send(index, value):
        rst[index] = value.astype(jnp.bfloat16)
        line_copy(index).start()

    theirs(3)
    theirs(1)
    far = mine(3)
    send(0, far[0:HALF])
    send(1, far[HALF:ROWS])
    theirs(2)
    above = mine(1)
    send(2, above[HALF:ROWS])
    own[0] = above[0:HALF]
    theirs(0)
    below = mine(2)
    send(3, below[0:HALF])
    own[1] = below[HALF:ROWS]
    for index in range(2):
        line_copy(index).wait_recv()
        send(4 + index, own[index] + rin[index].astype(jnp.float32))
    total = mine(0)
    scale = gate_ref[...].reshape(1, FEAT)
    for index, rows in ((3, slice(0, HALF)), (2, slice(HALF, ROWS))):
        line_copy(index).wait_recv()
        own[3 - index] = total[rows] + rin[index].astype(jnp.float32)
    for index, rows in ((4, slice(0, HALF)), (5, slice(HALF, ROWS))):
        line_copy(index).wait_recv()
        out_ref[rows, :] = ((own[index - 4] + rin[index].astype(jnp.float32)) * scale).astype(jnp.bfloat16)

    for ref, sem in (
        (kbuf.at[:, 0 : 6 * ROWS], kv_send.at[0]),
        (vbuf.at[:, 0 : 6 * ROWS], kv_send.at[1]),
        (qbuf.at[:, 0 : 7 * ROWS], q_send),
        (pbuf, o_send),
    ):
        pltpu.make_async_copy(ref, ref, sem).wait()

    for index in range(HEADS_Z):
        pair_copy(index).wait_send()
    for index in range(6):
        line_copy(index).wait_send()


def body(
    queries,
    window_keys,
    window_values,
    context_keys,
    context_values,
    block_group,
    sees,
    out_weight,
    gate,
):
    hbm = pl.BlockSpec(memory_space=pl.ANY)
    vmem = pl.BlockSpec(memory_space=pltpu.VMEM)
    dma = pltpu.SemaphoreType.DMA
    width = out_weight.shape[1]
    bf16 = jnp.bfloat16
    return pl.pallas_call(
        kernel,
        out_shape=jax.ShapeDtypeStruct((ROWS, FEAT), bf16),
        in_specs=[hbm] * 5 + [vmem, vmem, hbm, vmem],
        out_specs=vmem,
        scratch_shapes=[
            pltpu.VMEM((NH, QCH * ROWS, HD), bf16),
            pltpu.VMEM((NH, KEYS, HD), bf16),
            pltpu.VMEM((NH, KEYS, HD), bf16),
            pltpu.VMEM((MSG, KEYS), bf16),
            pltpu.VMEM((2, RING, KB, 2 * ROWS), jnp.float32),
            pltpu.VMEM((NH, QCH, MSG, HD), bf16),
            pltpu.VMEM((NH, 8, MSG, HD), bf16),
            pltpu.VMEM((4, ROWS, FEAT), bf16),
            pltpu.VMEM((FEAT, width), bf16),
            pltpu.VMEM((KEYS, 2 * ROWS), jnp.float32),
            pltpu.VMEM((KEYS, 2 * ROWS), jnp.float32),
            pltpu.VMEM((2, HEADS_Z, ROWS, FEAT), jnp.float32),
            pltpu.VMEM((HEADS_Z, ROWS, FEAT), bf16),
            pltpu.VMEM((HEADS_Z, ROWS, FEAT), bf16),
            pltpu.VMEM((2, HALF, FEAT), jnp.float32),
            pltpu.VMEM((6, HALF, FEAT), bf16),
            pltpu.VMEM((6, HALF, FEAT), bf16),
            dma((NH,)),
            dma(()),
            dma((2,)),
            dma((NH, 3)),
            dma(()),
            dma((NH, 5)),
            dma(()),
            dma((NH, 4)),
            dma((HEADS_Z,)),
            dma((HEADS_Z,)),
            dma((6,)),
            dma((6,)),
        ],
        compiler_params=pltpu.CompilerParams(
            collective_id=0, has_side_effects=True, vmem_limit_bytes=56 * 1024 * 1024
        ),
    )(
        queries,
        window_keys,
        window_values,
        context_keys,
        context_values,
        block_group,
        sees,
        out_weight,
        gate,
    )


def solution(mesh):
    placed = (
        P("tm", "head"),
        P("tm", "head"),
        P("tm", "head"),
        P("tm", "head"),
        P("tm", "head"),
        P(),
        P(),
        P("head", None),
        P("head"),
    )
    return jax.shard_map(
        body, mesh=mesh, in_specs=placed, out_specs=P("tm", "head"), check_vma=False
    )
```

```python
import functools
import math

import jax
import jax.numpy as jnp
from jax import lax
from jax.experimental import pallas as pl
from jax.experimental.pallas import tpu as pltpu
from jax.sharding import PartitionSpec as P

HD = 128
BLOCK = 64
ROWS = 128
NH = 6
FEAT = NH * HD
RING = 4
KEYS = 2 * ROWS * RING
KB = KEYS // BLOCK
QCH = 2 * RING
MSG = HD + 16
HEADS_Z = 4
NBLK = 128
HALF = ROWS // 2
EARLY = 2
LATER = 4
TURN = 4
STRAIGHT = 3
BIG = 1e30
FLOOR = -1e29
MESH = pl.DeviceIdType.MESH
LOG2 = math.log2(math.e) / math.sqrt(HD)


def remote(src, dst, send, recv, **device):
    return pltpu.make_async_remote_copy(
        src_ref=src, dst_ref=dst, send_sem=send, recv_sem=recv, device_id=device, device_id_type=MESH
    )


class Plan:
    def __init__(self, *entries):
        self.entries = entries

    def __getitem__(self, index):
        src, dst, send, recv, peer = self.entries[index]
        return remote(src, dst, send, recv, tm=peer)

    def __len__(self):
        return len(self.entries)


def dot_nt(a, b):
    return lax.dot_general(a, b, (((1,), (1,)), ((), ())), preferred_element_type=jnp.float32)


def unpack(message):
    stats = message[HD:MSG, :].astype(jnp.float32)
    return (message[0:HD, :].astype(jnp.float32), stats[0:1, :], stats[1:2, :] + stats[2:3, :])


def merge(parts):
    peak = parts[0][1]
    for part in parts[1:]:
        peak = jnp.maximum(peak, part[1])
    numer = None
    total = None
    for part in parts:
        factor = jnp.exp2(part[1] - peak)
        numer = part[0] * factor if numer is None else numer + part[0] * factor
        total = part[2] * factor if total is None else total + part[2] * factor
    return (numer, peak, total)


def stat_rows(peak, total):
    high = total.astype(jnp.bfloat16).astype(jnp.float32)
    rows = lax.broadcasted_iota(jnp.int32, (MSG - HD, peak.shape[1]), 0)
    picked = jnp.where(rows == 0, peak, jnp.where(rows == 1, high, total - high))
    return picked.astype(jnp.bfloat16)


def kernel(
    q_hbm,
    wk_hbm,
    wv_hbm,
    ck_hbm,
    cv_hbm,
    group_ref,
    sees_ref,
    w_hbm,
    gate_ref,
    out_ref,
    qbuf,
    kbuf,
    vbuf,
    vt,
    pen,
    pbuf,
    ibuf,
    att,
    wbuf,
    sa,
    sb,
    acc,
    pst,
    pin,
    own,
    rst,
    rin,
    load_sem,
    w_sem,
    kv_send,
    kv_recv,
    q_send,
    q_recv,
    o_send,
    o_recv,
    p_send,
    p_recv,
    r_send,
    r_recv,
):
    t = lax.axis_index("tm")
    hd = lax.axis_index("head")
    x = t % 4
    s = (t // 4) % 2
    y = t // 8
    zl = hd // 2
    core = hd % 2
    flip = t + 4 - 8 * s
    other = hd + 1 - 2 * core
    z = s * HEADS_Z + zl

    def z_device(delta):
        place = (z + delta + 8) % 8
        return {"tm": t + (place // HEADS_Z - s) * 4, "head": (place % HEADS_Z) * 2 + core}

    def z_side(delta):
        return (((z + delta + 8) % 8) // HEADS_Z + s) % 2

    z_up = z_device(1)
    z_down = z_device(-1)

    def along(delta):
        return (t - x + (x + delta + 4) % 4, t + ((y + delta + 4) % 4 - y) * 8)

    x_up, y_up = along(1)
    x_down, y_down = along(-1)

    def kv_peer(par, up):
        a, b = (x_up, y_up) if up else (x_down, y_down)
        return a * (1 - par) + b * par

    def far_peer(par):
        a, b = along(2)
        return a * par + b * (1 - par)

    def q_peer(par, up):
        a, b = (x_up, y_up) if up else (x_down, y_down)
        return a * par + b * (1 - par)

    def loads(h):
        cols = pl.ds(pl.multiple_of(h * HD, HD), HD)
        return (
            pltpu.make_async_copy(q_hbm.at[:, cols], qbuf.at[h, 0:ROWS], load_sem.at[h]),
            pltpu.make_async_copy(ck_hbm.at[:, cols], kbuf.at[h, 0:ROWS], load_sem.at[h]),
            pltpu.make_async_copy(wk_hbm.at[:, cols], kbuf.at[h, ROWS : 2 * ROWS], load_sem.at[h]),
            pltpu.make_async_copy(cv_hbm.at[:, cols], vbuf.at[h, 0:ROWS], load_sem.at[h]),
            pltpu.make_async_copy(wv_hbm.at[:, cols], vbuf.at[h, ROWS : 2 * ROWS], load_sem.at[h]),
        )

    @pl.loop(0, NH)
    def _(h):
        for copy in loads(h):
            copy.start()

    w_copy = pltpu.make_async_copy(w_hbm, wbuf, w_sem)

    barrier = pltpu.get_barrier_semaphore()
    x_far, y_far = along(2)
    for peer in (x_up, x_down, y_up, y_down, flip, x_far, y_far):
        pl.semaphore_signal(barrier, inc=1, device_id={"tm": peer}, device_id_type=MESH)
    pl.semaphore_signal(barrier, inc=1, device_id={"head": other}, device_id_type=MESH)
    for device in (z_up, z_down):
        pl.semaphore_signal(barrier, inc=1, device_id=device, device_id_type=MESH)
    pl.semaphore_wait(barrier, 10)

    def kslot(buf, h, slot):
        return buf.at[h, slot * 2 * ROWS : (slot + 1) * 2 * ROWS]

    def chunk(h, index):
        return qbuf.at[h, index * ROWS : (index + 1) * ROWS]

    def kv_copies(h):
        up = kv_peer(h % 2, True)
        down = kv_peer(h % 2, False)
        def one(buf, src, dst, kind, arrival, peer):
            return (kslot(buf, h, src), kslot(buf, h, dst), kv_send.at[kind], kv_recv.at[h, arrival], peer)

        return Plan(
            one(kbuf, 0, 1, 0, 0, up),
            one(vbuf, 0, 3, 1, 1, down),
            one(vbuf, 0, 1, 1, 2, up),
            one(kbuf, 0, 3, 0, 2, down),
            one(kbuf, 1, 2, 0, 2, up),
            one(vbuf, 3, 2, 1, 2, down),
        )

    def q_copies(h):
        up = q_peer(h % 2, True)
        down = q_peer(h % 2, False)

        def one(src, dst, arrival, peer):
            return (chunk(h, src), chunk(h, dst), q_send, q_recv.at[h, arrival], peer)

        return Plan(
            one(0, 4, 0, flip),
            one(0, 1, 1, up),
            one(0, 3, 3, down),
            one(4, 7, 2, down),
            one(4, 5, 4, up),
            one(1, 2, 3, up),
            one(7, 6, 4, down),
            one(4, 6, 4, far_peer(h % 2)),
        )

    def o_copy(h, side, place):
        peer = (q_peer(h % 2, False), far_peer(h % 2), q_peer(h % 2, True))[place - 1]
        slot = side * 3 + place - 1
        return remote(
            pbuf.at[h, side * RING + place], ibuf.at[h, slot], o_send, o_recv.at[h, side], tm=peer
        )

    def o_flip(h, side):
        return remote(
            pbuf.at[h, RING * side],
            ibuf.at[h, 7 - side],
            o_send,
            o_recv.at[h, 3 - side],
            tm=flip,
        )

    def first(h):
        pltpu.make_async_copy(qbuf.at[h, 0 : 5 * ROWS], qbuf.at[h, 0 : 5 * ROWS], load_sem.at[h]).wait()
        q = q_copies(h)
        kv = kv_copies(h)
        for plan, indices in ((q, (0, 1, 2)), (kv, (0, 1, 2, 3))):
            for index in indices:
                plan[index].start()

    def second(h):
        q = q_copies(h)
        kv = kv_copies(h)
        kv[0].wait_recv()
        kv[4].start()
        kv[1].wait_recv()
        kv[5].start()
        q[1].wait_recv()
        q[5].start()
        q[0].wait_recv()
        q[3].start()
        q[4].start()

        @pl.when(h < STRAIGHT)
        def _():
            q[7].start()

    def third(h):
        q = q_copies(h)
        q[3].wait_recv()
        q[6].start()

    def attention(h):
        par = h % 2
        late = (h >= TURN).astype(jnp.int32)

        def arrived(ref, sem):
            pltpu.make_async_copy(ref, ref, sem).wait()

        def pair(h, arrival):
            ref = qbuf.at[h, 0 : 2 * ROWS]
            arrived(ref, q_recv.at[h, arrival])

        def score(index, dest):
            block = (index + 2 * late) % 4
            queries = qbuf[h, pl.ds(pl.multiple_of(block * 2 * ROWS, 2 * ROWS), 2 * ROWS), :]
            dest[...] = dot_nt(kbuf[h], queries)

        def weigh(index, source):
            block = (index + 2 * late) % 4
            scores = source[...].reshape(KB, BLOCK, 2 * ROWS)
            hidden = pen[par, block]
            tops = jnp.max(scores, axis=1) * LOG2 - hidden
            peak = jnp.maximum(jnp.max(tops, axis=0, keepdims=True), FLOOR)
            peak = peak.astype(jnp.bfloat16).astype(jnp.float32)
            shift = peak + hidden
            weights = jnp.exp2(scores * LOG2 - shift[:, None, :]).astype(jnp.bfloat16)
            result = jnp.dot(
                vt[...], weights.reshape(KEYS, 2 * ROWS), preferred_element_type=jnp.float32
            )
            numer = result[0:HD, :].astype(jnp.bfloat16)
            stats = stat_rows(peak, result[HD : HD + 1, :])
            for half in range(2):
                lanes = slice(half * ROWS, (half + 1) * ROWS)
                pbuf[h, block * 2 + half, 0:HD, :] = numer[:, lanes]
                pbuf[h, block * 2 + half, HD:MSG, :] = stats[:, lanes]

        arrived(kbuf.at[h], kv_recv.at[h, 2])
        pair(h, 3)

        @pl.when(late == 1)
        def _():
            pair(h, 4)

        vt[0:HD, :] = vbuf[h].T
        score(0, sa)
        score(1, sb)
        weigh(0, sa)

        @pl.when(h == 0)
        def _():
            second(2)
            first(4)

        @pl.when(late == 0)
        def _():
            pair(h, 4)

        @pl.when(h < STRAIGHT)
        def _():
            arrived(chunk(h, 7), q_recv.at[h, 2])

        score(2, sa)
        weigh(1, sb)
        for place in (2, 3, 1):
            o_copy(h, late, place).start()
        score(3, sb)
        weigh(2, sa)
        weigh(3, sb)
        for place in (2, 3, 1):
            o_copy(h, 1 - late, place).start()

    def put(h, index, parts):
        numer, peak, total = merge(parts)
        pbuf[h, index, 0:HD, :] = numer.astype(jnp.bfloat16)
        pbuf[h, index, HD:MSG, :] = stat_rows(peak, total)

    def take(h, indices):
        return [unpack(ibuf[h, index]) for index in indices]

    def fold(h):
        o = o_copies(h)

        @pl.when(h < DIRECT)
        def _():
            for source, mine, nxt in ((0, 2, 4), (1, 7, 5)):
                o[source].wait_recv()
                put(h, mine, [unpack(pbuf[h, mine])] + take(h, (source,)))
                o[nxt].start()

    def cross(h):
        for side in (1, 0):
            landed = ibuf.at[h, side * 3 : side * 3 + 3]
            pltpu.make_async_copy(landed, landed, o_recv.at[h, side]).wait()
            put(h, RING * side, [unpack(pbuf[h, RING * side])] + take(h, range(side * 3, side * 3 + 3)))
            o_flip(h, side).start()

    def finish(h):
        cols = pl.ds(pl.multiple_of(h * HD, HD), HD)
        ready = []
        for side in range(2):
            o_flip(h, 1 - side).wait_recv()
            numer, peak, total = merge([unpack(pbuf[h, RING * side])] + take(h, (6 + side,)))
            ready.append((numer / total).T)
        mine, theirs = ready

        def chosen(delta):
            return jnp.where(z_side(delta) == 1, theirs, mine).astype(jnp.bfloat16)

        att[0, :, cols] = mine.astype(jnp.bfloat16)
        att[1, :, cols] = chosen(1)
        att[2, :, cols] = chosen(-1)
        att[3, 0:HALF, cols] = chosen(2)[0:HALF]
        att[3, HALF:ROWS, cols] = chosen(-2)[HALF:ROWS]

    def prepare():
        vt[HD:MSG, :] = jnp.ones((MSG - HD, KEYS), jnp.bfloat16)
        groups = sees_ref.shape[0]
        table = (
            (lax.broadcasted_iota(jnp.int32, (groups, NBLK), 0) == group_ref[...].reshape(1, NBLK))
            .astype(jnp.float32)
            .astype(jnp.bfloat16)
        )
        allowed = sees_ref[...].astype(jnp.float32).astype(jnp.bfloat16)
        for par in range(2):
            row = lax.broadcasted_iota(jnp.int32, (KB, NBLK), 0)
            slot = row // 4
            if par == 0:
                source = y * 8 + s * 4 + (x + 4 - slot) % 4
            else:
                source = ((y + 4 - slot) % 4) * 8 + s * 4 + x
            key_block = source * 2 + row % 2 + ((row // 2) % 2) * (NBLK // 2)
            picks = (
                (lax.broadcasted_iota(jnp.int32, (KB, NBLK), 1) == key_block)
                .astype(jnp.float32)
                .astype(jnp.bfloat16)
            )
            key_group = dot_nt(picks, table).astype(jnp.bfloat16)
            seen_by = dot_nt(key_group, allowed).astype(jnp.bfloat16)
            for place in range(RING):
                lane = lax.broadcasted_iota(jnp.int32, (NBLK, 2 * ROWS), 1)
                shift = 2 * (place % 2) + lane // ROWS
                side = 1 - s if place >= 2 else s
                if par == 0:
                    origin = ((y + 4 - shift) % 4) * 8 + side * 4 + x
                else:
                    origin = y * 8 + side * 4 + (x + 4 - shift) % 4
                query_block = NBLK // 2 + origin * 2 + (lane // BLOCK) % 2
                wanted = (
                    (lax.broadcasted_iota(jnp.int32, (NBLK, 2 * ROWS), 0) == query_block)
                    .astype(jnp.float32)
                    .astype(jnp.bfloat16)
                )
                query_group = jnp.dot(table, wanted, preferred_element_type=jnp.float32).astype(
                    jnp.bfloat16
                )
                visible = jnp.dot(seen_by, query_group, preferred_element_type=jnp.float32)
                pen[par, place] = jnp.where(visible > 0.5, 0.0, BIG)

    first(0)
    first(1)
    prepare()
    w_copy.start()
    first(2)
    second(0)
    first(3)
    second(1)

    def project(index, side, low, high):
        turn = index + (index // 2) * (5 - 2 * index)
        block = 2 * ((zl + turn) % HEADS_Z) + side
        cols = pl.ds(pl.multiple_of(block * FEAT, FEAT), FEAT)
        rows = slice(low * HD, high * HD)
        return jnp.dot(att[index, :, rows], wbuf[rows, cols], preferred_element_type=jnp.float32)

    def begin(side):
        @pl.loop(0, HEADS_Z)
        def _(index):
            acc[side, index] = project(index, side, 0, EARLY)

    def extend(side):
        @pl.loop(0, HEADS_Z)
        def _(index):
            acc[side, index] += project(index, side, EARLY, LATER)

    def start_projection(h):
        w_copy.wait()
        begin(0)
        begin(1)

    def go_on_projection(h):
        extend(0)
        extend(1)

    stages = (
        (third, -1, STRAIGHT, NH),
        (attention, 0, 0, NH),
        (first, -5, 5, NH),
        (second, -3, 3, NH),
        (start_projection, 1, NH - 1, NH),
        (cross, 2, 0, 1),
        (cross, 1, 1, NH),
        (finish, 3, 0, NH),
        (go_on_projection, 1, NH - 1, NH),
    )

    @pl.loop(0, NH + 3)
    def _(it):
        for stage, lag, low, high in stages:
            @pl.when((it >= lag + low) & (it < high + lag))
            def _():
                stage(it - lag)

    def pair_copy(index):
        return remote(pst.at[index], pin.at[index], p_send.at[index], p_recv.at[index], head=other)

    def line_copy(index):
        device = z_up if index % 2 == 0 else z_down
        return remote(rst.at[index], rin.at[index], r_send.at[index], r_recv.at[index], **device)

    def theirs(index):
        part = acc[1 - core, index] + project(index, 1 - core, LATER, NH)
        pst[index] = part.astype(jnp.bfloat16)
        pair_copy(index).start()

    def mine(index):
        part = acc[core, index] + project(index, core, LATER, NH)
        pair_copy(index).wait_recv()
        return part + pin[index].astype(jnp.float32)

    def send(index, value):
        rst[index] = value.astype(jnp.bfloat16)
        line_copy(index).start()

    theirs(3)
    theirs(1)
    far = mine(3)
    send(0, far[0:HALF])
    send(1, far[HALF:ROWS])
    theirs(2)
    above = mine(1)
    send(2, above[HALF:ROWS])
    own[0] = above[0:HALF]
    theirs(0)
    below = mine(2)
    send(3, below[0:HALF])
    own[1] = below[HALF:ROWS]
    for index in range(2):
        line_copy(index).wait_recv()
        send(4 + index, own[index] + rin[index].astype(jnp.float32))
    total = mine(0)
    scale = gate_ref[...].reshape(1, FEAT)
    for index, rows in ((3, slice(0, HALF)), (2, slice(HALF, ROWS))):
        line_copy(index).wait_recv()
        own[3 - index] = total[rows] + rin[index].astype(jnp.float32)
    for index, rows in ((4, slice(0, HALF)), (5, slice(HALF, ROWS))):
        line_copy(index).wait_recv()
        out_ref[rows, :] = ((own[index - 4] + rin[index].astype(jnp.float32)) * scale).astype(jnp.bfloat16)

    for ref, sem in (
        (kbuf.at[:, 0 : 6 * ROWS], kv_send.at[0]),
        (vbuf.at[:, 0 : 6 * ROWS], kv_send.at[1]),
        (qbuf.at[:, 0 : 7 * ROWS], q_send),
        (pbuf, o_send),
    ):
        pltpu.make_async_copy(ref, ref, sem).wait()

    for index in range(HEADS_Z):
        pair_copy(index).wait_send()
    for index in range(6):
        line_copy(index).wait_send()


def body(
    queries,
    window_keys,
    window_values,
    context_keys,
    context_values,
    block_group,
    sees,
    out_weight,
    gate,
):
    hbm = pl.BlockSpec(memory_space=pl.ANY)
    vmem = pl.BlockSpec(memory_space=pltpu.VMEM)
    dma = pltpu.SemaphoreType.DMA
    width = out_weight.shape[1]
    bf16 = jnp.bfloat16
    return pl.pallas_call(
        kernel,
        out_shape=jax.ShapeDtypeStruct((ROWS, FEAT), bf16),
        in_specs=[hbm] * 5 + [vmem, vmem, hbm, vmem],
        out_specs=vmem,
        scratch_shapes=[
            pltpu.VMEM((NH, QCH * ROWS, HD), bf16),
            pltpu.VMEM((NH, KEYS, HD), bf16),
            pltpu.VMEM((NH, KEYS, HD), bf16),
            pltpu.VMEM((MSG, KEYS), bf16),
            pltpu.VMEM((2, RING, KB, 2 * ROWS), jnp.float32),
            pltpu.VMEM((NH, QCH, MSG, HD), bf16),
            pltpu.VMEM((NH, 8, MSG, HD), bf16),
            pltpu.VMEM((4, ROWS, FEAT), bf16),
            pltpu.VMEM((FEAT, width), bf16),
            pltpu.VMEM((KEYS, 2 * ROWS), jnp.float32),
            pltpu.VMEM((KEYS, 2 * ROWS), jnp.float32),
            pltpu.VMEM((2, HEADS_Z, ROWS, FEAT), jnp.float32),
            pltpu.VMEM((HEADS_Z, ROWS, FEAT), bf16),
            pltpu.VMEM((HEADS_Z, ROWS, FEAT), bf16),
            pltpu.VMEM((2, HALF, FEAT), jnp.float32),
            pltpu.VMEM((6, HALF, FEAT), bf16),
            pltpu.VMEM((6, HALF, FEAT), bf16),
            dma((NH,)),
            dma(()),
            dma((2,)),
            dma((NH, 3)),
            dma(()),
            dma((NH, 5)),
            dma(()),
            dma((NH, 4)),
            dma((HEADS_Z,)),
            dma((HEADS_Z,)),
            dma((6,)),
            dma((6,)),
        ],
        compiler_params=pltpu.CompilerParams(
            collective_id=0, has_side_effects=True, vmem_limit_bytes=56 * 1024 * 1024
        ),
    )(
        queries,
        window_keys,
        window_values,
        context_keys,
        context_values,
        block_group,
        sees,
        out_weight,
        gate,
    )


def solution(mesh):
    placed = (
        P("tm", "head"),
        P("tm", "head"),
        P("tm", "head"),
        P("tm", "head"),
        P("tm", "head"),
        P(),
        P(),
        P("head", None),
        P("head"),
    )
    return jax.shard_map(
        body, mesh=mesh, in_specs=placed, out_specs=P("tm", "head"), check_vma=False
    )
```
